32 devices in a mesh: row: 4 (over z), col: 2 (over x), rep: 4 (over y, core).
Axes of the slice: x: 2, y: 2, z: 4, core: 2. Of those that a mesh axis runs over, the one named last changes fastest.
Arguments:
- features: bfloat16 [8192, 256], P(('col', 'rep'), 'row'), may hold values from -6 to 6
- weight: bfloat16 [256, 256], replicated, may hold values from -0.375 to 0.375
- cotangent: bfloat16 [8192, 256], P(('row', 'col', 'rep')), may hold values from -6 to 6
- block_values: bfloat16 [4, 8, 128, 128, 128], P('row', ('col', 'rep')), may hold values from -0.0625 to 0.0625
- block_coords: int32 [4, 8, 128, 2], P('row', ('col', 'rep')), may hold values from 0 to 15, as said below
- block_counts: int32 [4, 8], P('row', ('col', 'rep')), may hold values from 1 to 128, as said below
Outputs:
- activations: bfloat16 [8192, 256], P(('row', 'col', 'rep'))
- input_grad: bfloat16 [8192, 256], P(('col', 'rep'), 'row')
- weight_grad: float32 [256, 256], replicated
The draws below stay inside these ranges and needn't reach their ends.
Inputs may be any that keep to these rules, and one draw needn't show every extreme that they name: `block_coords`: each slot's row block is below 16 and its column block below 8. `block_counts`: some tile uses all 128 slots.
All inputs are finite; a program needn't handle non-finite values.
Results may differ from the reference program's by a relative error of at most 0.014.
Values may be sent and summed in bfloat16 or wider, within the bound.
A program may use at most 128 MiB of HBM per device.

```python
import jax
import jax.numpy as jnp
from jax import lax

F = 256
NODE_DEV = 256
NODES = 8192
ROW_TILES = 4
COL_TILES = 8
TILE_RB = 16
TILE_CB = 8
NNZB = 128


def draw_block_coords(key, part):
    key_rows = jax.random.fold_in(key, 11)
    key_cols = jax.random.fold_in(key, 12)
    rows_at = jax.random.randint(key_rows, (ROW_TILES, COL_TILES, NNZB), 0, TILE_RB, dtype=jnp.int32)
    cols_at = jax.random.randint(key_cols, (ROW_TILES, COL_TILES, NNZB), 0, TILE_CB, dtype=jnp.int32)
    rows_at = rows_at.at[0, 0, 0].set(TILE_RB - 1)
    cols_at = cols_at.at[0, 0, 0].set(TILE_CB - 1)
    return jnp.stack([rows_at, cols_at], axis=-1)


def draw_block_counts(key, part):
    key_counts = jax.random.fold_in(key, 21)
    key_full = jax.random.fold_in(key, 22)
    lowest = max(1, NNZB // 8)
    counts = jax.random.randint(key_counts, (ROW_TILES * COL_TILES,), lowest, NNZB + 1, dtype=jnp.int32)
    full_at = jax.random.randint(key_full, (), 0, ROW_TILES * COL_TILES, dtype=jnp.int32)
    counts = counts.at[full_at].set(NNZB)
    return counts.reshape(ROW_TILES, COL_TILES)


def levels(rng, extent, split, smallest, high):
    loudness, own = 1.0, jax.random.fold_in(rng, 6)
    for dim, shards_of in split:
        draws = jnp.exp(jax.random.uniform(jax.random.fold_in(own, dim), (shards_of,), jnp.float32, smallest / len(split), high / len(split)))
        loudness = loudness * jnp.repeat(draws, extent[dim] // shards_of).reshape([-1 if axis == dim else 1 for axis in range(len(extent))])
    return loudness


def bell_draw(key, shape, width, bound, cuts=(), kind=jnp.bfloat16):
    level = levels(key, shape, cuts, -0.22, 0.18) if cuts else 1.0
    drawn = jax.random.normal(key, shape, jnp.float32) * width * level
    return jnp.minimum(jnp.maximum(drawn, -bound), bound).astype(kind)


def setup_inputs(seed: int = 0) -> dict:
    seeds = jax.random.split(jax.random.key(seed), 7)
    features = bell_draw(seeds[0], (NODES, F), 1.0, 6.0, ((0, 8), (1, 4)))
    weight = bell_draw(seeds[1], (F, F), F ** -0.5, 0.375)
    cotangent = bell_draw(seeds[2], (NODES, F), 1.0, 6.0, ((0, 32),))
    block_values = bell_draw(seeds[3], (ROW_TILES, COL_TILES, NNZB, 128, 128), (16384 * NNZB // NODE_DEV) ** -0.5, 0.0625, ((0, 4), (1, 8)))
    block_coords = draw_block_coords(jax.random.fold_in(seeds[6], 71), 0)
    block_counts = draw_block_counts(jax.random.fold_in(seeds[6], 71), 0)
    return {"features": features, "weight": weight, "cotangent": cotangent, "block_values": block_values, "block_coords": block_coords, "block_counts": block_counts}


def reference(features, weight, cotangent, block_values, block_coords, block_counts):
    tiles_total = ROW_TILES * COL_TILES
    blocks = block_values.reshape(tiles_total, NNZB, 128, 128)
    coords = block_coords.reshape(tiles_total, NNZB, 2)
    counts = block_counts.reshape(tiles_total)
    tile_ids = jnp.arange(tiles_total, dtype=jnp.int32)
    slot_ids = jnp.arange(NNZB, dtype=jnp.int32)
    feat_blocks = features.reshape(NODES // 128, 128, F)

    def places(coords_t, tile):
        tile_row = tile // COL_TILES
        tile_col = tile % COL_TILES
        rows_at = (tile_row * TILE_RB + coords_t[:, 0]).astype(jnp.int32)
        cols_at = (tile_col * TILE_CB + coords_t[:, 1]).astype(jnp.int32)
        return rows_at, cols_at

    def forward_step(total, inputs):
        blocks_t, coords_t, count_t, tile = inputs
        rows_at, cols_at = places(coords_t, tile)
        chosen = feat_blocks[cols_at].astype(jnp.float32)
        product = jnp.einsum("bij,bjf->bif", blocks_t.astype(jnp.float32), chosen,
                             precision=lax.Precision.HIGHEST)
        is_live = (slot_ids < count_t).astype(jnp.float32)
        return total.at[rows_at].add(product * is_live[:, None, None]), None

    start = jnp.zeros((NODES // 128, 128, F), jnp.float32)
    total, _ = lax.scan(forward_step, start, (blocks, coords, counts, tile_ids))
    aggregate = total.reshape(NODES, F).astype(jnp.bfloat16)
    pre_act = jnp.dot(aggregate, weight, preferred_element_type=jnp.float32)
    sigma = jax.nn.sigmoid(pre_act)
    activations = (pre_act * sigma).astype(jnp.bfloat16)
    grad_pre = (cotangent.astype(jnp.float32) * sigma * (1.0 + pre_act * (1.0 - sigma))).astype(jnp.bfloat16)
    weight_grad = jnp.dot(aggregate.T, grad_pre, preferred_element_type=jnp.float32)
    back_rows = jnp.dot(grad_pre, weight.T, preferred_element_type=jnp.float32).astype(jnp.bfloat16)
    back_blocks = back_rows.reshape(NODES // 128, 128, F)

    def backward_step(total, inputs):
        blocks_t, coords_t, count_t, tile = inputs
        rows_at, cols_at = places(coords_t, tile)
        chosen = back_blocks[rows_at].astype(jnp.float32)
        product = jnp.einsum("bji,bjf->bif", blocks_t.astype(jnp.float32), chosen,
                             precision=lax.Precision.HIGHEST)
        is_live = (slot_ids < count_t).astype(jnp.float32)
        return total.at[cols_at].add(product * is_live[:, None, None]), None

    total_back, _ = lax.scan(backward_step, start, (blocks, coords, counts, tile_ids))
    input_grad = total_back.reshape(NODES, F).astype(jnp.bfloat16)
    return (activations, input_grad, weight_grad)
```

```python
import functools
import math

import jax
import jax.numpy as jnp
from jax import lax
from jax.experimental import pallas as pl
from jax.experimental.pallas import tpu as pltpu
from jax.sharding import PartitionSpec as P


def local_xla(features, weight, cotangent, block_values, block_coords, block_counts):
    blocks = block_values[0, 0]
    coords = block_coords[0, 0]
    live_count = block_counts[0, 0]
    slots = blocks.shape[0]
    gathered = lax.all_gather(features, "row", axis=1, tiled=True)
    feat_width = gathered.shape[1]
    col_blocks = gathered.shape[0] // 128
    row_blocks = cotangent.shape[0] * lax.axis_size(("col", "rep")) // 128
    feat_blocks = gathered.reshape(col_blocks, 128, feat_width)
    is_live = (jnp.arange(slots, dtype=jnp.int32) < live_count).astype(jnp.float32)
    per_turn = math.gcd(slots, 64)
    rounds = slots // per_turn
    pieces = (
        blocks.reshape(rounds, per_turn, 128, 128),
        coords[:, 0].reshape(rounds, per_turn),
        coords[:, 1].reshape(rounds, per_turn),
        is_live.reshape(rounds, per_turn),
    )

    def forward_step(total, piece):
        blocks_g, rows_g, cols_g, live_g = piece
        chosen = feat_blocks[cols_g]
        product = jnp.einsum("bij,bjf->bif", blocks_g, chosen, preferred_element_type=jnp.float32)
        return (total.at[rows_g].add(product * live_g[:, None, None]), None)

    partial_value, _ = lax.scan(
        forward_step, jnp.zeros((row_blocks, 128, feat_width), jnp.float32), pieces
    )
    partial_value = partial_value.reshape(row_blocks * 128, feat_width)
    summed = lax.psum_scatter(partial_value, ("col", "rep"), scatter_dimension=0, tiled=True)
    aggregate = summed.astype(jnp.bfloat16)
    pre_act = jnp.dot(aggregate, weight, preferred_element_type=jnp.float32)
    sigma = jax.nn.sigmoid(pre_act)
    activations = (pre_act * sigma).astype(jnp.bfloat16)
    grad_pre = (cotangent.astype(jnp.float32) * sigma * (1.0 + pre_act * (1.0 - sigma))).astype(
        jnp.bfloat16
    )
    weight_terms = jnp.dot(aggregate.T, grad_pre, preferred_element_type=jnp.float32)
    share = lax.psum_scatter(
        weight_terms.astype(jnp.bfloat16), ("col", "rep"), scatter_dimension=0, tiled=True
    ).astype(jnp.float32)
    share = lax.psum(share, "row")
    weight_grad = lax.all_gather(share, ("col", "rep"), axis=0, tiled=True)
    back_rows = jnp.dot(grad_pre, weight.T, preferred_element_type=jnp.float32).astype(jnp.bfloat16)
    back_all = lax.all_gather(back_rows, ("col", "rep"), axis=0, tiled=True)
    back_blocks = back_all.reshape(row_blocks, 128, back_all.shape[1])

    def backward_step(total, piece):
        blocks_g, rows_g, cols_g, live_g = piece
        chosen = back_blocks[rows_g]
        product = jnp.einsum("bji,bjf->bif", blocks_g, chosen, preferred_element_type=jnp.float32)
        return (total.at[cols_g].add(product * live_g[:, None, None]), None)

    grad_terms, _ = lax.scan(
        backward_step, jnp.zeros((col_blocks, 128, back_all.shape[1]), jnp.float32), pieces
    )
    grad_terms = grad_terms.reshape(col_blocks * 128, back_all.shape[1])
    input_grad = lax.psum_scatter(
        grad_terms.astype(jnp.bfloat16), "row", scatter_dimension=1, tiled=True
    )
    return (activations, input_grad, weight_grad)


BF16 = jnp.bfloat16
F32 = jnp.float32
VMEM_BUDGET = 60 * 2**20
MESH = pl.DeviceIdType.MESH


def dot(a, b, ca=1, cb=0):
    return lax.dot_general(a, b, (((ca,), (cb,)), ((), ())), preferred_element_type=F32)


def layer_kernel(
    sizes,
    count_hbm,
    coords_hbm,
    feat_hbm,
    weight_hbm,
    cot_hbm,
    blocks_hbm,
    act_hbm,
    igrad_hbm,
    wgrad_hbm,
    act_out,
    igrad_out,
    wgrad_out,
    count_in,
    coords_in,
    weight_in,
    cot_in,
    fbuf,
    bbuf,
    sums,
    dense,
    pbuf,
    prec,
    ownp,
    qbuf,
    qrec,
    held,
    agg,
    own_back,
    bown,
    brec,
    bpar,
    total,
    zbuf,
    zrec,
    wbuf,
    wrec,
    wrow,
    wall,
    tvec,
    table,
    load_sem,
    in_sem,
    t_sem,
    f_sem,
    p_sem,
    q_sem,
    b_sem,
    o_sem,
    c_sem,
    z_sem,
    w_sem,
    s_sem,
    g_sem,
):
    nrow, ncol, nrep = sizes
    nh = nrep // 2
    group = ncol * nrep
    every = nrow * group
    slots = bbuf.shape[0]
    nodes, width = act_out.shape
    fw, col_nodes = igrad_out.shape
    pieces, cw = fbuf.shape[1], fbuf.shape[3]
    row_blocks, col_blocks = dense.shape[0] // 128, dense.shape[1] // 128
    r, c, p = lax.axis_index("row"), lax.axis_index("col"), lax.axis_index("rep")
    h, k = p // 2, p % 2
    g = c * nrep + p
    me = r * group + g
    partner = h * 2 + (1 - k)
    offsets = [(dc, dh) for dc in reversed(range(ncol)) for dh in reversed(range(nh))]
    chips = len(offsets)
    far = chips - 1
    last = nrow - 1
    at_end = (r == 0) | (r == last)

    def to_row(j):
        return {"row": (r + j) % nrow}

    def to_group(j):
        q = (g + j) % group
        return {"col": q // nrep, "rep": q % nrep}

    def to_any(j):
        q = (me + j) % every
        return {"row": q // group, "col": q % group // nrep, "rep": q % nrep}

    def to_chip(i):
        dc, dh = offsets[i]
        return {"col": (c + dc) % ncol, "rep": ((h + dh) % nh) * 2 + k}

    def part_to(i, core):
        dc, dh = offsets[i]
        return ((c + dc) % ncol) * nrep + ((h + dh) % nh) * 2 + core

    def part_from(i, core):
        dc, dh = offsets[i]
        return ((c + ncol - dc) % ncol) * nrep + ((h + nh - dh) % nh) * 2 + core

    def by_row(choices):
        value = choices[0]
        for q in range(1, nrow):
            value = jnp.where(r == q, choices[q], value)
        return value

    def nearest(n):
        return by_row([sorted(range(nrow), key=lambda t: (abs(t - q), t))[n] for q in range(nrow)])

    def turns(q):
        if q in (0, last):
            return sorted(range(nrow), key=lambda t: -abs(t - q))
        late = {1: last, last - 1: 0}.get(q)
        rest = [t for t in range(nrow) if t not in (q, late)]
        rest.sort(key=lambda t: (abs(t - q), abs(2 * t - last)))
        return rest + ([] if late is None else [late]) + [q]

    def turn(n):
        return by_row([turns(q)[n] for q in range(nrow)])

    def rcopy(src, dst, sems, n, device):
        return pltpu.make_async_remote_copy(
            src_ref=src,
            dst_ref=dst,
            send_sem=sems.at[0],
            recv_sem=sems.at[n + 1],
            device_id=device,
            device_id_type=MESH,
        )

    def await_all(ref, sem):
        pltpu.make_async_copy(ref, ref, sem).wait()

    barrier = pltpu.get_barrier_semaphore()
    for j in range(1, nrow):
        pl.semaphore_signal(barrier, inc=1, device_id=to_row(j), device_id_type=MESH)
    for j in range(1, group):
        pl.semaphore_signal(barrier, inc=1, device_id=to_group(j), device_id_type=MESH)

    def span(j):
        return slice(j * cw, (j + 1) * cw)

    feats = [
        pltpu.make_async_copy(feat_hbm.at[:, span(j)], fbuf.at[r, j], in_sem.at[0]) for j in range(pieces)
    ]
    others = [
        pltpu.make_async_copy(src, dst, in_sem.at[n + 1])
        for n, (src, dst) in enumerate(
            [
                (coords_hbm, coords_in),
                (count_hbm, count_in),
                (weight_hbm, weight_in),
                (cot_hbm, cot_in),
            ]
        )
    ]
    for copy in feats + others[:2]:
        copy.start()
    chunks = load_sem.shape[0]
    per = slots // chunks
    loads = []
    for i in range(chunks):
        there = pl.ds(i * per, per)
        loads.append(pltpu.make_async_copy(blocks_hbm.at[there], bbuf.at[there], load_sem.at[i]))
        loads[-1].start()
    for copy in others[2:]:
        copy.start()
    pl.semaphore_wait(barrier, nrow - 1 + group - 1)

    def feat_copy(src, slot, j, step):
        target = {"row": (r + nrow + step) % nrow}
        return rcopy(src, fbuf.at[slot, j], f_sem, slot * pieces + j, target)

    for j in range(pieces):
        for step, there in ((1, r < last), (-1, r > 0)):
            pl.when(there)(feat_copy(feat_hbm.at[:, span(j)], r, j, step).start)

    def relay(d, j):
        for slot, step, there in (
            (jnp.maximum(r - d, 0), 1, (r >= d) & (r < last)),
            (jnp.minimum(r + d, last), -1, (r + d <= last) & (r > 0)),
        ):

            @pl.when(there)
            def _(slot=slot, step=step):
                copy = feat_copy(fbuf.at[slot, j], slot, j, step)
                copy.wait_recv()
                copy.start()

    for copy in others[:2]:
        copy.wait()
    await_all(fbuf.at[r], in_sem.at[0])
    places = row_blocks * col_blocks
    live = count_in[0, 0]
    row_form = coords_in[0:1, :] * col_blocks + coords_in[1:2, :]
    column_form = jnp.broadcast_to(row_form, (slots, slots)).T
    mine_at = lax.broadcasted_iota(jnp.int32, (slots, slots), 0)
    other_at = lax.broadcasted_iota(jnp.int32, (slots, slots), 1)
    hit = (column_form == row_form) & (mine_at < jnp.minimum(other_at, live))
    tvec[0:1, 0:slots] = jnp.max(jnp.where(hit, mine_at + 1, 0), axis=0, keepdims=True)
    for start in range(0, places, slots):
        hit = (column_form == other_at + start) & (mine_at < live)
        tvec[0:1, slots + start : 2 * slots + start] = jnp.max(
            jnp.where(hit, mine_at + 1, 0), axis=0, keepdims=True
        )
    tcopy = pltpu.make_async_copy(tvec, table, t_sem)
    tcopy.start()
    tcopy.wait()

    sums[0] = jnp.zeros((128, 128), F32)
    for i in range(chunks):
        loads[i].wait()

        def add_slot(s, carry):
            sums[s + 1] = sums[table[0, s]] + bbuf[s].astype(F32)
            return carry

        lax.fori_loop(i * per, (i + 1) * per, add_slot, 0)

    def fill(rb, carry):
        for cb in range(col_blocks):
            block = sums[table[0, slots + rb * col_blocks + cb]]
            dense[pl.ds(rb * 128, 128), cb * 128 : (cb + 1) * 128] = block.astype(BF16)
        return carry

    lax.fori_loop(0, row_blocks, fill, 0)

    def partials(n, core):
        slot = nearest(n)
        rows = jnp.concatenate([fbuf[slot, j] for j in range(pieces)], axis=1)
        parts = [part_to(i, core) for i in range(chips)]
        return [dot(rows, dense[pl.ds(part * nodes, nodes), :], 1, 1) for part in parts]

    def merge(n):
        pcopies[n].wait_recv()
        for i in range(chips):
            both = ownp[n, i] + prec[n, i].astype(F32)
            if i == far:
                held[n] = both
            else:
                qbuf[n, i] = both.astype(BF16)
                rcopy(qbuf.at[n, i], qrec.at[n, i], q_sem, n, to_chip(i)).start()

    def collect(n):
        await_all(qrec.at[n], q_sem.at[n + 1])
        got = held[n]
        for i in range(far):
            got = got + qrec[n, i].astype(F32)
        agg[nearest(n)] = got.astype(BF16)

    relays = [(d, j) for d in range(1, nrow - 1) for j in range(pieces)]
    when = [min(n if n < 3 else n - 1, 2 * nrow - 2) for n in range(len(relays))]
    pcopies = []
    for n in range(nrow):
        for half in range(2):
            for at, (d, j) in zip(when, relays):
                if at == 2 * n + half:
                    relay(d, j)
            if half == 0:
                if n > 0:
                    slot = nearest(n)
                    for j in range(pieces):
                        copy = feat_copy(fbuf.at[slot, j], slot, j, 0)
                        pl.when(at_end)(copy.wait_recv)
                for i, part in enumerate(partials(n, 1 - k)):
                    pbuf[n, i] = part.astype(BF16)
                pcopies.append(rcopy(pbuf.at[n], prec.at[n], p_sem, n, {"rep": partner}))
                pcopies[n].start()
            else:
                for i, part in enumerate(partials(n, k)):
                    ownp[n, i] = part
                merge(n)
                if n > 1:
                    collect(n - 2)

    for copy in others[2:]:
        copy.wait()
    collect(last - 1)
    collect(last)

    aggregate = agg[...].reshape(width, nodes)
    pre_act = dot(aggregate, weight_in[...], 0, 0)
    sigma = jax.nn.sigmoid(pre_act)
    grad_pre = (cot_in[...].astype(F32) * sigma * (1.0 + pre_act * (1.0 - sigma))).astype(BF16)
    own_back[...] = dot(weight_in[...], grad_pre, 1, 1).astype(BF16).reshape(nrow, fw, nodes)

    def spread(n):
        for i in range(far):
            rcopy(own_back.at[turn(n)], brec.at[n, i], b_sem, n * far + i, to_chip(i)).start()

    ocopy = rcopy(own_back, bown, o_sem, 0, {"rep": partner})
    ocopy.start()
    spread(0)
    terms = dot(aggregate, grad_pre).astype(BF16)
    tr, tl = wbuf.shape[1:]
    wbuf[...] = jnp.concatenate(
        [terms[:, n * tl : (n + 1) * tl].reshape(width // tr, tr, tl) for n in range(width // tl)], axis=0
    )
    for j in range(1, every):
        rcopy(wbuf.at[(me + j) % every], wrec.at[j - 1], w_sem, 0, to_any(j)).start()
    for n in range(1, nrow):
        spread(n)
    act_out[...] = (pre_act * sigma).astype(BF16)
    results = [
        pltpu.make_async_copy(src, dst, in_sem.at[5 + n])
        for n, (src, dst) in enumerate(
            [(act_out, act_hbm), (igrad_out, igrad_hbm), (wgrad_out, wgrad_hbm)]
        )
    ]
    results[0].start()

    def back_term(piece_t, part):
        return dot(piece_t, dense[pl.ds(part * nodes, nodes), :])

    def begin(n):
        total[n] = back_term(own_back[turn(n)], g) + back_term(bown[turn(n)], c * nrep + partner)

    def middle(n):
        for i in reversed(range(far)):
            copy = rcopy(brec.at[n, i], bpar.at[n, i], c_sem, n, {"rep": partner})
            await_all(brec.at[n, i], b_sem.at[n * far + i + 1])
            copy.start()
            total[n] += back_term(brec[n, i], part_from(i, k))

    def finish(n):
        await_all(bpar.at[n], c_sem.at[n + 1])
        for i in reversed(range(far)):
            total[n] += back_term(bpar[n, i], part_from(i, 1 - k))

    halves = zbuf.shape[1]
    fh = fw // halves

    def zpart(n, m):
        return total[n, m * fh : (m + 1) * fh]

    def zcopy(n, m):
        q = turn(n)
        far_off = jnp.abs(q - r) == last
        inner = jnp.where(r == 0, 1, last - 1)
        lane = jnp.where(far_off, nrow, r)
        target = {"row": jnp.where(far_off, inner, q)}
        return rcopy(zbuf.at[n, m], zrec.at[lane, m], z_sem, lane + jnp.where(far_off, m, 0), target)

    joins = (r == 1) | (r == last - 1)
    ocopy.wait_recv()
    begin(0)
    for n in range(nrow):
        middle(n)
        if n < last:
            begin(n + 1)
        finish(n)
        if n < last:
            for m in range(halves):
                there = None if n < last - 1 else jnp.logical_not(joins)

                def put(n=n, m=m):
                    zbuf[n, m] = zpart(n, m).astype(BF16)
                    zcopy(n, m).start()

                if there is None:
                    put()
                else:
                    pl.when(there)(put)
        if n == 0:
            await_all(wrec, w_sem.at[1])
            share = wbuf[me].astype(F32)
            for j in range(every - 1):
                share = share + wrec[j].astype(F32)
            wrow[r] = share.astype(BF16)
            for j in range(1, nrow):
                rcopy(wrow.at[r], wrow.at[r], s_sem, 0, to_row(j)).start()

    for m in range(halves):

        @pl.when(joins)
        def _(m=m):
            await_all(zrec.at[nrow, m], z_sem.at[nrow + m + 1])
            zbuf[last - 1, m] = (zpart(last - 1, m) + zrec[nrow, m].astype(F32)).astype(BF16)
            zcopy(last - 1, m).start()

    await_all(wrow.at[pl.ds(0, last)], s_sem.at[1])
    wall[g] = wrow[...]
    for j in range(1, group):
        rcopy(wrow, wall.at[g], g_sem, 0, to_group(j)).start()

    for j in range(1, nrow):
        q = (r + j) % nrow

        @pl.when(jnp.abs(q - r) < last)
        def _(q=q):
            await_all(zrec.at[q], z_sem.at[q + 1])
            for m in range(halves):
                total[last, m * fh : (m + 1) * fh] += zrec[q, m].astype(F32)

    igrad_out[...] = total[last].astype(BF16)
    results[1].start()
    await_all(wall.at[pl.ds(0, group - 1)], g_sem.at[1])
    per_lane = width // tr
    for row in range(nrow):
        for q in range(group):
            n = row * group + q
            at, lane = n % per_lane * tr, n // per_lane * tl
            wgrad_out[at : at + tr, lane : lane + tl] = wall[q, row].astype(F32)
    results[2].start()
    pl.when(at_end)(lambda: await_all(fbuf.at[0], f_sem.at[0]))
    pl.when(jnp.logical_not(at_end))(lambda: await_all(zrec, f_sem.at[0]))
    await_all(pbuf, p_sem.at[0])
    await_all(qbuf, q_sem.at[0])
    await_all(brec, b_sem.at[0])
    await_all(own_back, o_sem.at[0])
    await_all(bpar, c_sem.at[0])
    await_all(zbuf, z_sem.at[0])
    await_all(wrec, w_sem.at[0])
    await_all(wrow.at[pl.ds(0, last)], s_sem.at[0])
    await_all(wall.at[pl.ds(0, group - 1)], g_sem.at[0])
    for copy in results:
        copy.wait()


def keep_kernel(a_in, b_in, c_in, a_out, b_out, c_out, sem):
    copies = [
        pltpu.make_async_copy(src, dst, sem.at[n])
        for n, (src, dst) in enumerate([(c_in, c_out), (a_in, a_out), (b_in, b_out)])
    ]
    for copy in copies:
        copy.start()
    for copy in copies:
        copy.wait()


def local_kernel(sizes, features, weight, cotangent, block_values, block_coords, block_counts):
    nrow, ncol, nrep = sizes
    group = ncol * nrep
    every = nrow * group
    chips = group // 2
    blocks = block_values[0, 0]
    slots = blocks.shape[0]
    nodes, width = cotangent.shape
    col_nodes, fw = features.shape
    row_blocks = nodes * group // 128
    places = row_blocks * (col_nodes // 128)
    chunks = math.gcd(slots, 4)
    pieces = math.gcd(col_nodes // 128, 4)
    vmem = functools.partial(pl.BlockSpec, memory_space=pltpu.VMEM)
    hbm = functools.partial(pl.BlockSpec, memory_space=pl.ANY)
    dma = pltpu.SemaphoreType.DMA
    block = (fw, nodes)
    tile = (width * width // every // 128, 128)
    outs = pl.pallas_call(
        functools.partial(layer_kernel, sizes),
        out_shape=(
            pltpu.VMEM((nodes, width), BF16),
            pltpu.VMEM((fw, col_nodes), BF16),
            pltpu.VMEM((width, width), F32),
        ),
        in_specs=[hbm()] * 6,
        out_specs=(hbm(), hbm(), hbm()),
        scratch_shapes=[
            pltpu.VMEM((nodes, width), BF16),
            pltpu.VMEM((fw, col_nodes), BF16),
            pltpu.VMEM((width, width), F32),
            pltpu.SMEM((1, 1), jnp.int32),
            pltpu.VMEM((2, slots), jnp.int32),
            pltpu.VMEM((width, width), BF16),
            pltpu.VMEM((nodes, width), BF16),
            pltpu.VMEM((nrow, pieces, fw, col_nodes // pieces), BF16),
            pltpu.VMEM((slots, 128, 128), BF16),
            pltpu.VMEM((slots + 1, 128, 128), F32),
            pltpu.VMEM((row_blocks * 128, col_nodes), BF16),
            pltpu.VMEM((nrow, chips) + block, BF16),
            pltpu.VMEM((nrow, chips) + block, BF16),
            pltpu.VMEM((nrow, chips) + block, F32),
            pltpu.VMEM((nrow, chips - 1) + block, BF16),
            pltpu.VMEM((nrow, chips - 1) + block, BF16),
            pltpu.VMEM((nrow,) + block, F32),
            pltpu.VMEM((nrow,) + block, BF16),
            pltpu.VMEM((nrow,) + block, BF16),
            pltpu.VMEM((nrow,) + block, BF16),
            pltpu.VMEM((nrow, chips - 1) + block, BF16),
            pltpu.VMEM((nrow, chips - 1) + block, BF16),
            pltpu.VMEM((nrow, fw, col_nodes), F32),
            pltpu.VMEM((nrow - 1, 2, fw // 2, col_nodes), BF16),
            pltpu.VMEM((nrow + 1, 2, fw // 2, col_nodes), BF16),
            pltpu.VMEM((every,) + tile, BF16),
            pltpu.VMEM((every - 1,) + tile, BF16),
            pltpu.VMEM((nrow,) + tile, BF16),
            pltpu.VMEM((group, nrow) + tile, BF16),
            pltpu.VMEM((1, slots + places), jnp.int32),
            pltpu.SMEM((1, slots + places), jnp.int32),
            dma((chunks,)),
            dma((8,)),
            dma,
            dma((1 + nrow * pieces,)),
            dma((1 + nrow,)),
            dma((1 + nrow,)),
            dma((1 + nrow * (chips - 1),)),
            dma((2,)),
            dma((1 + nrow,)),
            dma((3 + nrow,)),
            dma((2,)),
            dma((2,)),
            dma((2,)),
        ],
        compiler_params=pltpu.CompilerParams(
            collective_id=0, has_side_effects=True, vmem_limit_bytes=VMEM_BUDGET
        ),
    )(block_counts, block_coords[0, 0].T, features.T, weight, cotangent, blocks)
    activations, input_grad_t, weight_grad = pl.pallas_call(
        keep_kernel,
        out_shape=tuple(jax.ShapeDtypeStruct(x.shape, x.dtype) for x in outs),
        in_specs=[hbm()] * 3,
        out_specs=(hbm(),) * 3,
        scratch_shapes=[dma((3,))],
    )(*[pltpu.with_memory_space_constraint(x, pltpu.VMEM) for x in outs])
    return activations, input_grad_t.T, weight_grad


def fits(mesh, features, weight, cotangent, block_values):
    nrow, ncol, nrep = (mesh.shape[name] for name in ("row", "col", "rep"))
    group = ncol * nrep
    width = features.shape[1]
    fw = width // nrow
    rows, cols = cotangent.shape[0] // nrow, features.shape[0] // group
    tile = rows * cols * 2 + block_values.shape[2] * 128 * 128 * 6
    moved = 8 * rows * width + 12 * cols * width
    whole = nrep % 2 == 0 and block_values.shape[2] == 128 and rows * cols % 128**3 == 0
    whole = whole and fw % 32 == 0 and width % 128 == 0 and width**2 % (2048 * nrow * group) == 0
    return whole and nrow > 3 and group > 2 and tile + moved < VMEM_BUDGET * 3 // 4


def solution(mesh):
    in_specs = (
        P(("col", "rep"), "row"),
        P(),
        P(("row", "col", "rep"), None),
        P("row", ("col", "rep"), None, None, None),
        P("row", ("col", "rep"), None, None),
        P("row", ("col", "rep")),
    )
    out_specs = (P(("row", "col", "rep"), None), P(("col", "rep"), "row"), P())
    sizes = tuple(mesh.shape[name] for name in ("row", "col", "rep"))

    def run(features, weight, cotangent, block_values, block_coords, block_counts):
        if fits(mesh, features, weight, cotangent, block_values):
            body = functools.partial(local_kernel, sizes)
        else:
            body = local_xla
        return jax.shard_map(
            body, mesh=mesh, in_specs=in_specs, out_specs=out_specs, check_vma=False
        )(features, weight, cotangent, block_values, block_coords, block_counts)

    return run
```

```python
import functools
import math

import jax
import jax.numpy as jnp
from jax import lax
from jax.experimental import pallas as pl
from jax.experimental.pallas import tpu as pltpu
from jax.sharding import PartitionSpec as P


def local_xla(features, weight, cotangent, block_values, block_coords, block_counts):
    blocks = block_values[0, 0]
    coords = block_coords[0, 0]
    live_count = block_counts[0, 0]
    slots = blocks.shape[0]
    gathered = lax.all_gather(features, "row", axis=1, tiled=True)
    feat_width = gathered.shape[1]
    col_blocks = gathered.shape[0] // 128
    row_blocks = cotangent.shape[0] * lax.axis_size(("col", "rep")) // 128
    feat_blocks = gathered.reshape(col_blocks, 128, feat_width)
    is_live = (jnp.arange(slots, dtype=jnp.int32) < live_count).astype(jnp.float32)
    per_turn = math.gcd(slots, 64)
    rounds = slots // per_turn
    pieces = (
        blocks.reshape(rounds, per_turn, 128, 128),
        coords[:, 0].reshape(rounds, per_turn),
        coords[:, 1].reshape(rounds, per_turn),
        is_live.reshape(rounds, per_turn),
    )

    def forward_step(total, piece):
        blocks_g, rows_g, cols_g, live_g = piece
        chosen = feat_blocks[cols_g]
        product = jnp.einsum("bij,bjf->bif", blocks_g, chosen, preferred_element_type=jnp.float32)
        return (total.at[rows_g].add(product * live_g[:, None, None]), None)

    partial_value, _ = lax.scan(
        forward_step, jnp.zeros((row_blocks, 128, feat_width), jnp.float32), pieces
    )
    partial_value = partial_value.reshape(row_blocks * 128, feat_width)
    summed = lax.psum_scatter(partial_value, ("col", "rep"), scatter_dimension=0, tiled=True)
    aggregate = summed.astype(jnp.bfloat16)
    pre_act = jnp.dot(aggregate, weight, preferred_element_type=jnp.float32)
    sigma = jax.nn.sigmoid(pre_act)
    activations = (pre_act * sigma).astype(jnp.bfloat16)
    grad_pre = (cotangent.astype(jnp.float32) * sigma * (1.0 + pre_act * (1.0 - sigma))).astype(
        jnp.bfloat16
    )
    weight_terms = jnp.dot(aggregate.T, grad_pre, preferred_element_type=jnp.float32)
    share = lax.psum_scatter(
        weight_terms.astype(jnp.bfloat16), ("col", "rep"), scatter_dimension=0, tiled=True
    ).astype(jnp.float32)
    share = lax.psum(share, "row")
    weight_grad = lax.all_gather(share, ("col", "rep"), axis=0, tiled=True)
    back_rows = jnp.dot(grad_pre, weight.T, preferred_element_type=jnp.float32).astype(jnp.bfloat16)
    back_all = lax.all_gather(back_rows, ("col", "rep"), axis=0, tiled=True)
    back_blocks = back_all.reshape(row_blocks, 128, back_all.shape[1])

    def backward_step(total, piece):
        blocks_g, rows_g, cols_g, live_g = piece
        chosen = back_blocks[rows_g]
        product = jnp.einsum("bji,bjf->bif", blocks_g, chosen, preferred_element_type=jnp.float32)
        return (total.at[cols_g].add(product * live_g[:, None, None]), None)

    grad_terms, _ = lax.scan(
        backward_step, jnp.zeros((col_blocks, 128, back_all.shape[1]), jnp.float32), pieces
    )
    grad_terms = grad_terms.reshape(col_blocks * 128, back_all.shape[1])
    input_grad = lax.psum_scatter(
        grad_terms.astype(jnp.bfloat16), "row", scatter_dimension=1, tiled=True
    )
    return (activations, input_grad, weight_grad)


BF16 = jnp.bfloat16
F32 = jnp.float32
VMEM_BUDGET = 60 * 2**20
MESH = pl.DeviceIdType.MESH


def dot(a, b, ca=1, cb=0):
    return lax.dot_general(a, b, (((ca,), (cb,)), ((), ())), preferred_element_type=F32)


def layer_kernel(
    sizes,
    count_hbm,
    coords_hbm,
    feat_hbm,
    weight_hbm,
    cot_hbm,
    blocks_hbm,
    act_hbm,
    igrad_hbm,
    wgrad_hbm,
    act_out,
    igrad_out,
    wgrad_out,
    count_in,
    coords_in,
    weight_in,
    cot_in,
    fbuf,
    bbuf,
    sums,
    dense,
    pbuf,
    prec,
    ownp,
    accp,
    acco,
    qbuf,
    qrec,
    held,
    agg,
    own_back,
    bown,
    brec,
    bpar,
    total,
    zbuf,
    zrec,
    wbuf,
    wrec,
    wrow,
    wall,
    tvec,
    table,
    load_sem,
    in_sem,
    t_sem,
    f_sem,
    p_sem,
    q_sem,
    b_sem,
    o_sem,
    c_sem,
    z_sem,
    w_sem,
    s_sem,
    g_sem,
):
    nrow, ncol, nrep = sizes
    nh = nrep // 2
    group = ncol * nrep
    every = nrow * group
    slots = bbuf.shape[0]
    nodes, width = act_out.shape
    fw, col_nodes = igrad_out.shape
    pieces, cw = fbuf.shape[1], fbuf.shape[3]
    row_blocks, col_blocks = dense.shape[0] // 128, dense.shape[1] // 128
    r, c, p = lax.axis_index("row"), lax.axis_index("col"), lax.axis_index("rep")
    h, k = p // 2, p % 2
    g = c * nrep + p
    me = r * group + g
    partner = h * 2 + (1 - k)
    offsets = [(dc, dh) for dc in reversed(range(ncol)) for dh in reversed(range(nh))]
    chips = len(offsets)
    far = chips - 1
    last = nrow - 1
    at_end = (r == 0) | (r == last)
    joints = [(1, last, last - 1), (last - 1, 0, 1)]

    def to_row(j):
        return {"row": (r + j) % nrow}

    def to_group(j):
        q = (g + j) % group
        return {"col": q // nrep, "rep": q % nrep}

    def to_any(j):
        q = (me + j) % every
        return {"row": q // group, "col": q % group // nrep, "rep": q % nrep}

    def to_chip(i):
        dc, dh = offsets[i]
        return {"col": (c + dc) % ncol, "rep": ((h + dh) % nh) * 2 + k}

    def part_to(i, core):
        dc, dh = offsets[i]
        return ((c + dc) % ncol) * nrep + ((h + dh) % nh) * 2 + core

    def part_from(i, core):
        dc, dh = offsets[i]
        return ((c + ncol - dc) % ncol) * nrep + ((h + nh - dh) % nh) * 2 + core

    def by_row(choices):
        value = choices[0]
        for q in range(1, nrow):
            value = jnp.where(r == q, choices[q], value)
        return value

    def nearest(n):
        return by_row([sorted(range(nrow), key=lambda t: (abs(t - q), t))[n] for q in range(nrow)])

    def turns(q):
        rest = [t for t in range(nrow) if t != q]
        if q == 0:
            return rest[::-1] + [q]
        if q == last:
            return [0] + rest[:0:-1] + [q]
        rest.sort(key=lambda t: (abs(t - q), abs(2 * t - last)))
        for row, passed, n in joints:
            if row == q:
                rest.remove(passed)
                rest.insert(n, passed)
        return rest + [q]

    def turn(n):
        return by_row([turns(q)[n] for q in range(nrow)])

    def rcopy(src, dst, sems, n, device):
        return pltpu.make_async_remote_copy(
            src_ref=src,
            dst_ref=dst,
            send_sem=sems.at[0],
            recv_sem=sems.at[n + 1],
            device_id=device,
            device_id_type=MESH,
        )

    def await_all(ref, sem):
        pltpu.make_async_copy(ref, ref, sem).wait()

    def span(j):
        return slice(j * cw, (j + 1) * cw)

    feats = [
        pltpu.make_async_copy(feat_hbm.at[:, span(j)], fbuf.at[r, j], in_sem.at[0]) for j in range(pieces)
    ]
    others = [
        pltpu.make_async_copy(src, dst, in_sem.at[n + 1])
        for n, (src, dst) in enumerate(
            [
                (coords_hbm, coords_in),
                (count_hbm, count_in),
                (weight_hbm, weight_in),
                (cot_hbm, cot_in),
            ]
        )
    ]
    for copy in feats:
        copy.start()

    barrier = pltpu.get_barrier_semaphore()
    for j in range(1, nrow):
        pl.semaphore_signal(barrier, inc=1, device_id=to_row(j), device_id_type=MESH)
    for j in range(1, group):
        pl.semaphore_signal(barrier, inc=1, device_id=to_group(j), device_id_type=MESH)
    for copy in others[:2]:
        copy.start()
    chunks = load_sem.shape[0]
    per = slots // chunks
    loads = []
    for i in range(chunks):
        there = pl.ds(i * per, per)
        loads.append(pltpu.make_async_copy(blocks_hbm.at[there], bbuf.at[there], load_sem.at[i]))
        loads[-1].start()
    for copy in others[2:]:
        copy.start()
    await_all(fbuf.at[r], in_sem.at[0])
    pl.semaphore_wait(barrier, nrow - 1 + group - 1)

    def feat_copy(src, slot, j, step):
        target = {"row": (r + nrow + step) % nrow}
        return rcopy(src, fbuf.at[slot, j], f_sem, slot * pieces + j, target)

    for j in range(pieces):
        for step, there in ((1, r < last), (-1, r > 0)):
            pl.when(there)(feat_copy(fbuf.at[r, j], r, j, step).start)

    def relay(d, j):
        for slot, step, there in (
            (jnp.maximum(r - d, 0), 1, (r >= d) & (r < last)),
            (jnp.minimum(r + d, last), -1, (r + d <= last) & (r > 0)),
        ):

            @pl.when(there)
            def _(slot=slot, step=step):
                copy = feat_copy(fbuf.at[slot, j], slot, j, step)
                copy.wait_recv()
                copy.start()

    for copy in others[:2]:
        copy.wait()
    places = row_blocks * col_blocks
    live = count_in[0, 0]
    row_form = coords_in[0:1, :] * col_blocks + coords_in[1:2, :]
    column_form = jnp.broadcast_to(row_form, (slots, slots)).T
    mine_at = lax.broadcasted_iota(jnp.int32, (slots, slots), 0)
    other_at = lax.broadcasted_iota(jnp.int32, (slots, slots), 1)
    hit = (column_form == row_form) & (mine_at < jnp.minimum(other_at, live))
    tvec[0:1, 0:slots] = jnp.max(jnp.where(hit, mine_at + 1, 0), axis=0, keepdims=True)
    for start in range(0, places, slots):
        hit = (column_form == other_at + start) & (mine_at < live)
        tvec[0:1, slots + start : 2 * slots + start] = jnp.max(
            jnp.where(hit, mine_at + 1, 0), axis=0, keepdims=True
        )
    tcopy = pltpu.make_async_copy(tvec, table, t_sem)
    tcopy.start()
    tcopy.wait()

    sums[0] = jnp.zeros((128, 128), F32)
    for i in range(chunks):
        loads[i].wait()

        def add_slot(s, carry):
            sums[s + 1] = sums[table[0, s]] + bbuf[s].astype(F32)
            return carry

        lax.fori_loop(i * per, (i + 1) * per, add_slot, 0)

    def fill(rb, carry):
        for cb in range(col_blocks):
            block = sums[table[0, slots + rb * col_blocks + cb]]
            dense[pl.ds(rb * 128, 128), cb * 128 : (cb + 1) * 128] = block.astype(BF16)
        return carry

    lax.fori_loop(0, row_blocks, fill, 0)

    def partials(n, core, reach):
        slot, (low, high) = nearest(n), reach
        rows = jnp.concatenate([fbuf[slot, j] for j in range(low, high)], axis=1)
        parts = [part_to(i, core) for i in range(chips)]
        cols = slice(low * cw, high * cw)
        return [dot(rows, dense[pl.ds(part * nodes, nodes), cols], 1, 1) for part in parts]

    def tail(n):
        return (0 if n < last else pieces - 1, pieces)

    def merge(n):
        pcopies[n].wait_recv()
        for i in range(chips):
            both = ownp[n, i] + prec[n, i].astype(F32)
            if i == far:
                held[n] = both
            else:
                qbuf[n, i] = both.astype(BF16)
                rcopy(qbuf.at[n, i], qrec.at[n, i], q_sem, n, to_chip(i)).start()

    def collect(n):
        await_all(qrec.at[n], q_sem.at[n + 1])
        got = held[n]
        for i in range(far):
            got = got + qrec[n, i].astype(F32)
        agg[nearest(n)] = got.astype(BF16)

    relays = [(d, j) for d in range(1, nrow - 1) for j in range(pieces)]
    when = [min((0, 1, 2, 2, 3, 4, 4, 5)[n % 8] + n // 8 * 4, 2 * nrow - 2) for n in range(len(relays))]
    pcopies = []
    for n in range(nrow):
        for half in range(2):
            for at, (d, j) in zip(when, relays):
                if at == 2 * n + half:
                    relay(d, j)
            if half == 0:
                if n > 0:
                    slot = nearest(n)
                    for j in range(pieces):
                        copy = feat_copy(fbuf.at[slot, j], slot, j, 0)
                        pl.when(at_end)(copy.wait_recv)
                        if n == last and 0 < j < pieces - 1:
                            for core, sofar in ((1 - k, accp), (k, acco)):
                                for i, part in enumerate(partials(n, core, (0 if j == 1 else j, j + 1))):
                                    sofar[i] = part if j == 1 else sofar[i] + part
                for i, part in enumerate(partials(n, 1 - k, tail(n))):
                    pbuf[n, i] = (part if n < last else accp[i] + part).astype(BF16)
                pcopies.append(rcopy(pbuf.at[n], prec.at[n], p_sem, n, {"rep": partner}))
                pcopies[n].start()
            else:
                for i, part in enumerate(partials(n, k, tail(n))):
                    ownp[n, i] = part if n < last else acco[i] + part
                merge(n)
                if n > 1:
                    collect(n - 2)

    for copy in others[2:]:
        copy.wait()
    collect(last - 1)
    collect(last)

    aggregate = agg[...].reshape(width, nodes)
    pre_act = dot(aggregate, weight_in[...], 0, 0)
    sigma = jax.nn.sigmoid(pre_act)
    grad_pre = (cot_in[...].astype(F32) * sigma * (1.0 + pre_act * (1.0 - sigma))).astype(BF16)
    own_back[...] = dot(weight_in[...], grad_pre, 1, 1).astype(BF16).reshape(nrow, fw, nodes)

    units = [(0, m, fw // 2) for m in (0, fw // 2)] + [(n, 0, fw) for n in range(1, nrow)]

    def spread(u):
        n, at, size = units[u]
        rows = pl.ds(at, size)
        for i in range(far):
            src, dst = own_back.at[turn(n), rows], brec.at[n, i, rows]
            rcopy(src, dst, b_sem, u * far + i, to_chip(i)).start()

    ocopy = rcopy(own_back, bown, o_sem, 0, {"rep": partner})
    spread(0)
    ocopy.start()
    spread(1)
    terms = dot(aggregate, grad_pre).astype(BF16)
    tr, tl = wbuf.shape[1:]
    wbuf[...] = jnp.concatenate(
        [terms[:, n * tl : (n + 1) * tl].reshape(width // tr, tr, tl) for n in range(width // tl)], axis=0
    )
    for j in range(1, every):
        rcopy(wbuf.at[(me + j) % every], wrec.at[j - 1], w_sem, 0, to_any(j)).start()
    for u in range(2, len(units)):
        spread(u)
    act_out[...] = (pre_act * sigma).astype(BF16)
    results = [
        pltpu.make_async_copy(src, dst, in_sem.at[5 + n])
        for n, (src, dst) in enumerate(
            [(act_out, act_hbm), (igrad_out, igrad_hbm), (wgrad_out, wgrad_hbm)]
        )
    ]
    results[0].start()

    def back_term(piece_t, part):
        return dot(piece_t, dense[pl.ds(part * nodes, nodes), :])

    def begin(n):
        total[n] = back_term(own_back[turn(n)], g) + back_term(bown[turn(n)], c * nrep + partner)

    def middle(u):
        n, at, size = units[u]
        rows = pl.ds(at, size)
        for i in reversed(range(far)):
            copy = rcopy(brec.at[n, i, rows], bpar.at[n, i, rows], c_sem, u, {"rep": partner})
            await_all(brec.at[n, i, rows], b_sem.at[u * far + i + 1])
            copy.start()
            total[n, rows] += back_term(brec[n, i, rows], part_from(i, k))

    def finish(u):
        n, at, size = units[u]
        rows = pl.ds(at, size)
        await_all(bpar.at[n, :, rows], c_sem.at[u + 1])
        for i in reversed(range(far)):
            total[n, rows] += back_term(bpar[n, i, rows], part_from(i, 1 - k))

    steps = zbuf.shape[1]
    fh = fw // steps

    def zpart(n, m):
        return total[n, m * fh : (m + 1) * fh]

    def zcopy(n, m):
        q = turn(n)
        far_off = jnp.abs(q - r) == last
        inner = jnp.where(r == 0, 1, last - 1)
        lane = jnp.where(far_off, nrow, r)
        target = {"row": jnp.where(far_off, inner, q)}
        return rcopy(zbuf.at[n, m], zrec.at[lane, m], z_sem, lane + jnp.where(far_off, m, 0), target)

    ocopy.wait_recv()
    begin(0)

    def join(n, span):
        for row, _, at in joints:
            if at == n:

                @pl.when(r == row)
                def _():
                    for m in span:
                        await_all(zrec.at[nrow, m], z_sem.at[nrow + m + 1])
                        zbuf[n, m] = (zpart(n, m) + zrec[nrow, m].astype(F32)).astype(BF16)
                        zcopy(n, m).start()

    for u, (n, at, size) in enumerate(units):
        middle(u)
        if u > 0 and n < last:
            begin(n + 1)
        if u > 0 and n > 0:
            join(n - 1, range(steps // 2))
        finish(u)
        if n < last:

            def put(n=n, at=at, size=size):
                for m in range(at // fh, (at + size) // fh):
                    zbuf[n, m] = zpart(n, m).astype(BF16)
                    zcopy(n, m).start()

            keep = functools.reduce(jnp.logical_and, [r != row for row, _, at in joints if at == n], r >= 0)
            pl.when(keep)(put)
        if n > 0:
            join(n - 1, range(steps // 2, steps))
        if u == 1:
            await_all(wrec, w_sem.at[1])
            share = wbuf[me].astype(F32)
            for j in range(every - 1):
                share = share + wrec[j].astype(F32)
            wrow[r] = share.astype(BF16)
            for j in range(1, nrow):
                rcopy(wrow.at[r], wrow.at[r], s_sem, 0, to_row(j)).start()

    await_all(wrow.at[pl.ds(0, last)], s_sem.at[1])
    wall[g] = wrow[...]
    for j in range(1, group):
        rcopy(wrow, wall.at[g], g_sem, 0, to_group(j)).start()

    for j in range(1, nrow):
        q = (r + j) % nrow

        @pl.when(jnp.abs(q - r) < last)
        def _(q=q):
            await_all(zrec.at[q], z_sem.at[q + 1])
            for m in range(steps):
                total[last, m * fh : (m + 1) * fh] += zrec[q, m].astype(F32)

    igrad_out[...] = total[last].astype(BF16)
    results[1].start()
    await_all(wall.at[pl.ds(0, group - 1)], g_sem.at[1])
    per_lane = width // tr
    for row in range(nrow):
        for q in range(group):
            n = row * group + q
            at, lane = n % per_lane * tr, n // per_lane * tl
            wgrad_out[at : at + tr, lane : lane + tl] = wall[q, row].astype(F32)
    results[2].start()
    pl.when(at_end)(lambda: await_all(fbuf.at[0], f_sem.at[0]))
    pl.when(jnp.logical_not(at_end))(lambda: await_all(zrec, f_sem.at[0]))
    await_all(pbuf, p_sem.at[0])
    await_all(qbuf, q_sem.at[0])
    await_all(brec, b_sem.at[0])
    await_all(own_back, o_sem.at[0])
    await_all(bpar, c_sem.at[0])
    await_all(zbuf, z_sem.at[0])
    await_all(wrec, w_sem.at[0])
    await_all(wrow.at[pl.ds(0, last)], s_sem.at[0])
    await_all(wall.at[pl.ds(0, group - 1)], g_sem.at[0])
    for copy in results:
        copy.wait()


def keep_kernel(a_in, b_in, c_in, a_out, b_out, c_out, sem):
    copies = [
        pltpu.make_async_copy(src, dst, sem.at[n])
        for n, (src, dst) in enumerate([(c_in, c_out), (a_in, a_out), (b_in, b_out)])
    ]
    for copy in copies:
        copy.start()
    for copy in copies:
        copy.wait()


def local_kernel(sizes, features, weight, cotangent, block_values, block_coords, block_counts):
    nrow, ncol, nrep = sizes
    group = ncol * nrep
    every = nrow * group
    chips = group // 2
    blocks = block_values[0, 0]
    slots = blocks.shape[0]
    nodes, width = cotangent.shape
    col_nodes, fw = features.shape
    row_blocks = nodes * group // 128
    places = row_blocks * (col_nodes // 128)
    chunks = math.gcd(slots, 4)
    pieces = math.gcd(col_nodes // 128, 4)
    vmem = functools.partial(pl.BlockSpec, memory_space=pltpu.VMEM)
    hbm = functools.partial(pl.BlockSpec, memory_space=pl.ANY)
    dma = pltpu.SemaphoreType.DMA
    block = (fw, nodes)
    tile = (width * width // every // 128, 128)
    outs = pl.pallas_call(
        functools.partial(layer_kernel, sizes),
        out_shape=(
            pltpu.VMEM((nodes, width), BF16),
            pltpu.VMEM((fw, col_nodes), BF16),
            pltpu.VMEM((width, width), F32),
        ),
        in_specs=[pl.BlockSpec(memory_space=pltpu.HBM)] + [hbm()] * 5,
        out_specs=(hbm(), hbm(), hbm()),
        scratch_shapes=[
            pltpu.VMEM((nodes, width), BF16),
            pltpu.VMEM((fw, col_nodes), BF16),
            pltpu.VMEM((width, width), F32),
            pltpu.SMEM((1, 1), jnp.int32),
            pltpu.VMEM((2, slots), jnp.int32),
            pltpu.VMEM((width, width), BF16),
            pltpu.VMEM((nodes, width), BF16),
            pltpu.VMEM((nrow, pieces, fw, col_nodes // pieces), BF16),
            pltpu.VMEM((slots, 128, 128), BF16),
            pltpu.VMEM((slots + 1, 128, 128), F32),
            pltpu.VMEM((row_blocks * 128, col_nodes), BF16),
            pltpu.VMEM((nrow, chips) + block, BF16),
            pltpu.VMEM((nrow, chips) + block, BF16),
            pltpu.VMEM((nrow, chips) + block, F32),
            pltpu.VMEM((chips,) + block, F32),
            pltpu.VMEM((chips,) + block, F32),
            pltpu.VMEM((nrow, chips - 1) + block, BF16),
            pltpu.VMEM((nrow, chips - 1) + block, BF16),
            pltpu.VMEM((nrow,) + block, F32),
            pltpu.VMEM((nrow,) + block, BF16),
            pltpu.VMEM((nrow,) + block, BF16),
            pltpu.VMEM((nrow,) + block, BF16),
            pltpu.VMEM((nrow, chips - 1) + block, BF16),
            pltpu.VMEM((nrow, chips - 1) + block, BF16),
            pltpu.VMEM((nrow, fw, col_nodes), F32),
            pltpu.VMEM((nrow - 1, 4, fw // 4, col_nodes), BF16),
            pltpu.VMEM((nrow + 1, 4, fw // 4, col_nodes), BF16),
            pltpu.VMEM((every,) + tile, BF16),
            pltpu.VMEM((every - 1,) + tile, BF16),
            pltpu.VMEM((nrow,) + tile, BF16),
            pltpu.VMEM((group, nrow) + tile, BF16),
            pltpu.VMEM((1, slots + places), jnp.int32),
            pltpu.SMEM((1, slots + places), jnp.int32),
            dma((chunks,)),
            dma((8,)),
            dma,
            dma((1 + nrow * pieces,)),
            dma((1 + nrow,)),
            dma((1 + nrow,)),
            dma((1 + (nrow + 1) * (chips - 1),)),
            dma((2,)),
            dma((2 + nrow,)),
            dma((5 + nrow,)),
            dma((2,)),
            dma((2,)),
            dma((2,)),
        ],
        compiler_params=pltpu.CompilerParams(
            collective_id=0, has_side_effects=True, vmem_limit_bytes=VMEM_BUDGET
        ),
    )(block_counts, block_coords[0, 0].T, features.T, weight, cotangent, blocks)
    activations, input_grad_t, weight_grad = pl.pallas_call(
        keep_kernel,
        out_shape=tuple(jax.ShapeDtypeStruct(x.shape, x.dtype) for x in outs),
        in_specs=[hbm()] * 3,
        out_specs=(hbm(),) * 3,
        scratch_shapes=[dma((3,))],
    )(*[pltpu.with_memory_space_constraint(x, pltpu.VMEM) for x in outs])
    return activations, input_grad_t.T, weight_grad


def fits(mesh, features, weight, cotangent, block_values):
    nrow, ncol, nrep = (mesh.shape[name] for name in ("row", "col", "rep"))
    group = ncol * nrep
    width = features.shape[1]
    fw = width // nrow
    rows, cols = cotangent.shape[0] // nrow, features.shape[0] // group
    tile = rows * cols * 2 + block_values.shape[2] * 128 * 128 * 6
    moved = 8 * rows * width + 12 * cols * width
    whole = nrep % 2 == 0 and block_values.shape[2] == 128 and rows * cols % 128**3 == 0
    whole = whole and fw % 64 == 0 and width % 128 == 0 and width**2 % (2048 * nrow * group) == 0
    return whole and nrow > 3 and group > 2 and tile + moved < VMEM_BUDGET * 3 // 4


def solution(mesh):
    in_specs = (
        P(("col", "rep"), "row"),
        P(),
        P(("row", "col", "rep"), None),
        P("row", ("col", "rep"), None, None, None),
        P("row", ("col", "rep"), None, None),
        P("row", ("col", "rep")),
    )
    out_specs = (P(("row", "col", "rep"), None), P(("col", "rep"), "row"), P())
    sizes = tuple(mesh.shape[name] for name in ("row", "col", "rep"))

    def run(features, weight, cotangent, block_values, block_coords, block_counts):
        if fits(mesh, features, weight, cotangent, block_values):
            body = functools.partial(local_kernel, sizes)
        else:
            body = local_xla
        return jax.shard_map(
            body, mesh=mesh, in_specs=in_specs, out_specs=out_specs, check_vma=False
        )(features, weight, cotangent, block_values, block_coords, block_counts)

    return run
```

```python
import functools
import math

import jax
import jax.numpy as jnp
from jax import lax
from jax.experimental import pallas as pl
from jax.experimental.pallas import tpu as pltpu
from jax.sharding import PartitionSpec as P


def local_xla(features, weight, cotangent, block_values, block_coords, block_counts):
    blocks = block_values[0, 0]
    coords = block_coords[0, 0]
    live_count = block_counts[0, 0]
    slots = blocks.shape[0]
    gathered = lax.all_gather(features, "row", axis=1, tiled=True)
    feat_width = gathered.shape[1]
    col_blocks = gathered.shape[0] // 128
    row_blocks = cotangent.shape[0] * lax.axis_size(("col", "rep")) // 128
    feat_blocks = gathered.reshape(col_blocks, 128, feat_width)
    is_live = (jnp.arange(slots, dtype=jnp.int32) < live_count).astype(jnp.float32)
    per_turn = math.gcd(slots, 64)
    rounds = slots // per_turn
    pieces = (
        blocks.reshape(rounds, per_turn, 128, 128),
        coords[:, 0].reshape(rounds, per_turn),
        coords[:, 1].reshape(rounds, per_turn),
        is_live.reshape(rounds, per_turn),
    )

    def forward_step(total, piece):
        blocks_g, rows_g, cols_g, live_g = piece
        chosen = feat_blocks[cols_g]
        product = jnp.einsum("bij,bjf->bif", blocks_g, chosen, preferred_element_type=jnp.float32)
        return (total.at[rows_g].add(product * live_g[:, None, None]), None)

    partial_value, _ = lax.scan(
        forward_step, jnp.zeros((row_blocks, 128, feat_width), jnp.float32), pieces
    )
    partial_value = partial_value.reshape(row_blocks * 128, feat_width)
    summed = lax.psum_scatter(partial_value, ("col", "rep"), scatter_dimension=0, tiled=True)
    aggregate = summed.astype(jnp.bfloat16)
    pre_act = jnp.dot(aggregate, weight, preferred_element_type=jnp.float32)
    sigma = jax.nn.sigmoid(pre_act)
    activations = (pre_act * sigma).astype(jnp.bfloat16)
    grad_pre = (cotangent.astype(jnp.float32) * sigma * (1.0 + pre_act * (1.0 - sigma))).astype(
        jnp.bfloat16
    )
    weight_terms = jnp.dot(aggregate.T, grad_pre, preferred_element_type=jnp.float32)
    share = lax.psum_scatter(
        weight_terms.astype(jnp.bfloat16), ("col", "rep"), scatter_dimension=0, tiled=True
    ).astype(jnp.float32)
    share = lax.psum(share, "row")
    weight_grad = lax.all_gather(share, ("col", "rep"), axis=0, tiled=True)
    back_rows = jnp.dot(grad_pre, weight.T, preferred_element_type=jnp.float32).astype(jnp.bfloat16)
    back_all = lax.all_gather(back_rows, ("col", "rep"), axis=0, tiled=True)
    back_blocks = back_all.reshape(row_blocks, 128, back_all.shape[1])

    def backward_step(total, piece):
        blocks_g, rows_g, cols_g, live_g = piece
        chosen = back_blocks[rows_g]
        product = jnp.einsum("bji,bjf->bif", blocks_g, chosen, preferred_element_type=jnp.float32)
        return (total.at[cols_g].add(product * live_g[:, None, None]), None)

    grad_terms, _ = lax.scan(
        backward_step, jnp.zeros((col_blocks, 128, back_all.shape[1]), jnp.float32), pieces
    )
    grad_terms = grad_terms.reshape(col_blocks * 128, back_all.shape[1])
    input_grad = lax.psum_scatter(
        grad_terms.astype(jnp.bfloat16), "row", scatter_dimension=1, tiled=True
    )
    return (activations, input_grad, weight_grad)


BF16 = jnp.bfloat16
F32 = jnp.float32
VMEM_BUDGET = 60 * 2**20
MESH = pl.DeviceIdType.MESH


def dot(a, b, ca=1, cb=0):
    return lax.dot_general(a, b, (((ca,), (cb,)), ((), ())), preferred_element_type=F32)


def layer_kernel(
    sizes,
    count_hbm,
    coords_hbm,
    feat_hbm,
    weight_hbm,
    cot_hbm,
    blocks_hbm,
    act_hbm,
    igrad_hbm,
    wgrad_hbm,
    act_out,
    igrad_out,
    wgrad_out,
    count_in,
    coords_in,
    weight_in,
    cot_in,
    fbuf,
    bbuf,
    sums,
    dense,
    pbuf,
    prec,
    ownp,
    accp,
    acco,
    qbuf,
    qrec,
    held,
    agg,
    own_back,
    bown,
    brec,
    bpar,
    total,
    zbuf,
    zrec,
    wbuf,
    wrec,
    wrow,
    wall,
    tvec,
    table,
    load_sem,
    in_sem,
    t_sem,
    f_sem,
    p_sem,
    q_sem,
    b_sem,
    o_sem,
    c_sem,
    z_sem,
    w_sem,
    s_sem,
    g_sem,
):
    nrow, ncol, nrep = sizes
    nh = nrep // 2
    group = ncol * nrep
    every = nrow * group
    slots = bbuf.shape[0]
    nodes, width = act_out.shape
    fw, col_nodes = igrad_out.shape
    pieces, cw = fbuf.shape[1], fbuf.shape[3]
    row_blocks, col_blocks = dense.shape[0] // 128, dense.shape[1] // 128
    r, c, p = lax.axis_index("row"), lax.axis_index("col"), lax.axis_index("rep")
    h, k = p // 2, p % 2
    g = c * nrep + p
    me = r * group + g
    partner = h * 2 + (1 - k)
    offsets = [(dc, dh) for dc in reversed(range(ncol)) for dh in reversed(range(nh))]
    chips = len(offsets)
    far = chips - 1
    last = nrow - 1
    at_end = (r == 0) | (r == last)
    joints = [(1, last, last - 1), (last - 1, 0, 1)]

    def to_row(j):
        return {"row": (r + j) % nrow}

    def to_group(j):
        q = (g + j) % group
        return {"col": q // nrep, "rep": q % nrep}

    def to_any(j):
        q = (me + j) % every
        return {"row": q // group, "col": q % group // nrep, "rep": q % nrep}

    def to_chip(i):
        dc, dh = offsets[i]
        return {"col": (c + dc) % ncol, "rep": ((h + dh) % nh) * 2 + k}

    def part_to(i, core):
        dc, dh = offsets[i]
        return ((c + dc) % ncol) * nrep + ((h + dh) % nh) * 2 + core

    def part_from(i, core):
        dc, dh = offsets[i]
        return ((c + ncol - dc) % ncol) * nrep + ((h + nh - dh) % nh) * 2 + core

    def by_row(choices):
        value = choices[0]
        for q in range(1, nrow):
            value = jnp.where(r == q, choices[q], value)
        return value

    def nearest(n):
        return by_row([sorted(range(nrow), key=lambda t: (abs(t - q), t))[n] for q in range(nrow)])

    def turns(q):
        rest = [t for t in range(nrow) if t != q]
        if q == 0:
            return rest[::-1] + [q]
        if q == last:
            return [0] + rest[:0:-1] + [q]
        rest.sort(key=lambda t: (abs(t - q), abs(2 * t - last)))
        for row, passed, n in joints:
            if row == q:
                rest.remove(passed)
                rest.insert(n, passed)
        return rest + [q]

    def turn(n):
        return by_row([turns(q)[n] for q in range(nrow)])

    def rcopy(src, dst, sems, n, device):
        return pltpu.make_async_remote_copy(
            src_ref=src,
            dst_ref=dst,
            send_sem=sems.at[0],
            recv_sem=sems.at[n + 1],
            device_id=device,
            device_id_type=MESH,
        )

    def await_all(ref, sem):
        pltpu.make_async_copy(ref, ref, sem).wait()

    def span(j):
        return slice(j * cw, (j + 1) * cw)

    feats = [
        pltpu.make_async_copy(feat_hbm.at[:, span(j)], fbuf.at[r, j], in_sem.at[0]) for j in range(pieces)
    ]
    others = [
        pltpu.make_async_copy(src, dst, in_sem.at[n + 1])
        for n, (src, dst) in enumerate(
            [
                (coords_hbm, coords_in),
                (count_hbm, count_in),
                (weight_hbm, weight_in),
                (cot_hbm, cot_in),
            ]
        )
    ]
    for copy in feats:
        copy.start()

    barrier = pltpu.get_barrier_semaphore()
    for j in range(1, nrow):
        pl.semaphore_signal(barrier, inc=1, device_id=to_row(j), device_id_type=MESH)
    for j in range(1, group):
        pl.semaphore_signal(barrier, inc=1, device_id=to_group(j), device_id_type=MESH)
    for copy in others[:2]:
        copy.start()
    chunks = load_sem.shape[0]
    per = slots // chunks
    loads = []
    for i in range(chunks):
        there = pl.ds(i * per, per)
        loads.append(pltpu.make_async_copy(blocks_hbm.at[there], bbuf.at[there], load_sem.at[i]))
        loads[-1].start()
    for copy in others[2:]:
        copy.start()
    await_all(fbuf.at[r], in_sem.at[0])
    pl.semaphore_wait(barrier, nrow - 1 + group - 1)

    def feat_copy(src, slot, j, step):
        target = {"row": (r + nrow + step) % nrow}
        return rcopy(src, fbuf.at[slot, j], f_sem, slot * pieces + j, target)

    for j in range(pieces):
        for step, there in ((1, r < last), (-1, r > 0)):
            pl.when(there)(feat_copy(fbuf.at[r, j], r, j, step).start)

    def relay(d, j):
        for slot, step, there in (
            (jnp.maximum(r - d, 0), 1, (r >= d) & (r < last)),
            (jnp.minimum(r + d, last), -1, (r + d <= last) & (r > 0)),
        ):

            @pl.when(there)
            def _(slot=slot, step=step):
                copy = feat_copy(fbuf.at[slot, j], slot, j, step)
                copy.wait_recv()
                copy.start()

    for copy in others[:2]:
        copy.wait()
    places = row_blocks * col_blocks
    live = count_in[0, 0]
    row_form = coords_in[0:1, :] * col_blocks + coords_in[1:2, :]
    column_form = jnp.broadcast_to(row_form, (slots, slots)).T
    mine_at = lax.broadcasted_iota(jnp.int32, (slots, slots), 0)
    other_at = lax.broadcasted_iota(jnp.int32, (slots, slots), 1)
    hit = (column_form == row_form) & (mine_at < jnp.minimum(other_at, live))
    tvec[0:1, 0:slots] = jnp.max(jnp.where(hit, mine_at + 1, 0), axis=0, keepdims=True)
    for start in range(0, places, slots):
        hit = (column_form == other_at + start) & (mine_at < live)
        tvec[0:1, slots + start : 2 * slots + start] = jnp.max(
            jnp.where(hit, mine_at + 1, 0), axis=0, keepdims=True
        )
    tcopy = pltpu.make_async_copy(tvec, table, t_sem)
    tcopy.start()
    tcopy.wait()

    sums[0] = jnp.zeros((128, 128), F32)
    for i in range(chunks):
        loads[i].wait()

        def add_slot(s, carry):
            sums[s + 1] = sums[table[0, s]] + bbuf[s].astype(F32)
            return carry

        lax.fori_loop(i * per, (i + 1) * per, add_slot, 0)

    def fill(rb, carry):
        for cb in range(col_blocks):
            block = sums[table[0, slots + rb * col_blocks + cb]]
            dense[pl.ds(rb * 128, 128), cb * 128 : (cb + 1) * 128] = block.astype(BF16)
        return carry

    lax.fori_loop(0, row_blocks, fill, 0)

    def partials(n, core, reach):
        slot, (low, high) = nearest(n), reach
        rows = jnp.concatenate([fbuf[slot, j] for j in range(low, high)], axis=1)
        parts = [part_to(i, core) for i in range(chips)]
        cols = slice(low * cw, high * cw)
        return [dot(rows, dense[pl.ds(part * nodes, nodes), cols], 1, 1) for part in parts]

    def tail(n):
        return (0 if n < last else pieces - 1, pieces)

    def merge(n):
        pcopies[n].wait_recv()
        for i in range(chips):
            both = ownp[n, i] + prec[n, i].astype(F32)
            if i == far:
                held[n] = both
            else:
                qbuf[n, i] = both.astype(BF16)
                rcopy(qbuf.at[n, i], qrec.at[n, i], q_sem, n, to_chip(i)).start()

    def collect(n):
        await_all(qrec.at[n], q_sem.at[n + 1])
        got = held[n]
        for i in range(far):
            got = got + qrec[n, i].astype(F32)
        agg[nearest(n)] = got.astype(BF16)

    relays = [(d, j) for d in range(1, nrow - 1) for j in range(pieces)]
    when = [min((0, 1, 2, 2, 3, 4, 4, 5)[n % 8] + n // 8 * 4, 2 * nrow - 2) for n in range(len(relays))]
    pcopies = []
    for n in range(nrow):
        for half in range(2):
            for at, (d, j) in zip(when, relays):
                if at == 2 * n + half:
                    relay(d, j)
            if half == 0:
                if n > 0:
                    slot = nearest(n)
                    for j in range(pieces):
                        copy = feat_copy(fbuf.at[slot, j], slot, j, 0)
                        pl.when(at_end)(copy.wait_recv)
                        if n == last and 0 < j < pieces - 1:
                            for core, sofar in ((1 - k, accp), (k, acco)):
                                for i, part in enumerate(partials(n, core, (0 if j == 1 else j, j + 1))):
                                    sofar[i] = part if j == 1 else sofar[i] + part
                for i, part in enumerate(partials(n, 1 - k, tail(n))):
                    pbuf[n, i] = (part if n < last else accp[i] + part).astype(BF16)
                pcopies.append(rcopy(pbuf.at[n], prec.at[n], p_sem, n, {"rep": partner}))
                pcopies[n].start()
            else:
                for i, part in enumerate(partials(n, k, tail(n))):
                    ownp[n, i] = part if n < last else acco[i] + part
                merge(n)
                if n > 1:
                    collect(n - 2)

    for copy in others[2:]:
        copy.wait()
    collect(last - 1)
    collect(last)

    aggregate = agg[...].reshape(width, nodes)
    pre_act = dot(aggregate, weight_in[...], 0, 0)
    sigma = jax.nn.sigmoid(pre_act)
    grad_pre = (cot_in[...].astype(F32) * sigma * (1.0 + pre_act * (1.0 - sigma))).astype(BF16)
    own_back[...] = dot(weight_in[...], grad_pre, 1, 1).astype(BF16).reshape(nrow, fw, nodes)

    units = [(0, m, fw // 2) for m in (0, fw // 2)] + [(n, 0, fw) for n in range(1, nrow)]

    def spread(u):
        n, at, size = units[u]
        rows = pl.ds(at, size)
        for i in range(far):
            src, dst = own_back.at[turn(n), rows], brec.at[n, i, rows]
            rcopy(src, dst, b_sem, u * far + i, to_chip(i)).start()

    ocopy = rcopy(own_back, bown, o_sem, 0, {"rep": partner})
    spread(0)
    ocopy.start()
    spread(1)
    spread(2)
    terms = dot(aggregate, grad_pre).astype(BF16)
    tr, tl = wbuf.shape[1:]
    wbuf[...] = jnp.concatenate(
        [terms[:, n * tl : (n + 1) * tl].reshape(width // tr, tr, tl) for n in range(width // tl)], axis=0
    )
    for j in range(1, every):
        rcopy(wbuf.at[(me + j) % every], wrec.at[j - 1], w_sem, 0, to_any(j)).start()
    for u in range(3, len(units)):
        spread(u)
    act_out[...] = (pre_act * sigma).astype(BF16)
    results = [
        pltpu.make_async_copy(src, dst, in_sem.at[5 + n])
        for n, (src, dst) in enumerate(
            [(act_out, act_hbm), (igrad_out, igrad_hbm), (wgrad_out, wgrad_hbm)]
        )
    ]
    results[0].start()

    def back_term(piece_t, part):
        return dot(piece_t, dense[pl.ds(part * nodes, nodes), :])

    def begin(n):
        total[n] = back_term(own_back[turn(n)], g) + back_term(bown[turn(n)], c * nrep + partner)

    def middle(u):
        n, at, size = units[u]
        rows = pl.ds(at, size)
        for i in reversed(range(far)):
            copy = rcopy(brec.at[n, i, rows], bpar.at[n, i, rows], c_sem, u, {"rep": partner})
            await_all(brec.at[n, i, rows], b_sem.at[u * far + i + 1])
            copy.start()
            total[n, rows] += back_term(brec[n, i, rows], part_from(i, k))

    def finish(u):
        n, at, size = units[u]
        rows = pl.ds(at, size)
        await_all(bpar.at[n, :, rows], c_sem.at[u + 1])
        for i in reversed(range(far)):
            total[n, rows] += back_term(bpar[n, i, rows], part_from(i, 1 - k))

    steps = zbuf.shape[1]
    fh = fw // steps

    def zpart(n, m):
        return total[n, m * fh : (m + 1) * fh]

    def zcopy(n, m):
        q = turn(n)
        far_off = jnp.abs(q - r) == last
        inner = jnp.where(r == 0, 1, last - 1)
        lane = jnp.where(far_off, nrow, r)
        target = {"row": jnp.where(far_off, inner, q)}
        return rcopy(zbuf.at[n, m], zrec.at[lane, m], z_sem, lane + jnp.where(far_off, m, 0), target)

    ocopy.wait_recv()
    begin(0)

    def join(n, span):
        for row, _, at in joints:
            if at == n:

                @pl.when(r == row)
                def _():
                    for m in span:
                        await_all(zrec.at[nrow, m], z_sem.at[nrow + m + 1])
                        zbuf[n, m] = (zpart(n, m) + zrec[nrow, m].astype(F32)).astype(BF16)
                        zcopy(n, m).start()

    def advance(u):
        if u < len(units):
            if units[u][1] == 0 and u > 0:
                begin(units[u][0])
            middle(u)

    middle(0)
    for u, (n, at, size) in enumerate(units):
        pl.when(k == 1)(lambda: advance(u + 1))
        if u > 0 and n > 0:
            join(n - 1, range(steps // 2))
        finish(u)
        if n == 1:
            await_all(wrec, w_sem.at[1])
            share = wbuf[me].astype(F32)
            for j in range(every - 1):
                share = share + wrec[j].astype(F32)
            wrow[r] = share.astype(BF16)
            for j in range(1, nrow):
                rcopy(wrow.at[r], wrow.at[r], s_sem, 0, to_row(j)).start()
        if n < last:

            def put(n=n, at=at, size=size):
                for m in range(at // fh, (at + size) // fh):
                    zbuf[n, m] = zpart(n, m).astype(BF16)
                    zcopy(n, m).start()

            keep = functools.reduce(jnp.logical_and, [r != row for row, _, at in joints if at == n], r >= 0)
            pl.when(keep)(put)
        pl.when(k == 0)(lambda: advance(u + 1))
        if n > 0:
            join(n - 1, range(steps // 2, steps))

    await_all(wrow.at[pl.ds(0, last)], s_sem.at[1])
    wall[g] = wrow[...]
    for j in range(1, group):
        rcopy(wrow, wall.at[g], g_sem, 0, to_group(j)).start()

    for j in range(1, nrow):
        q = (r + j) % nrow

        @pl.when(jnp.abs(q - r) < last)
        def _(q=q):
            await_all(zrec.at[q], z_sem.at[q + 1])
            for m in range(steps):
                total[last, m * fh : (m + 1) * fh] += zrec[q, m].astype(F32)

    igrad_out[...] = total[last].astype(BF16)
    results[1].start()
    await_all(wall.at[pl.ds(0, group - 1)], g_sem.at[1])
    per_lane = width // tr
    for row in range(nrow):
        for q in range(group):
            n = row * group + q
            at, lane = n % per_lane * tr, n // per_lane * tl
            wgrad_out[at : at + tr, lane : lane + tl] = wall[q, row].astype(F32)
    results[2].start()
    pl.when(at_end)(lambda: await_all(fbuf.at[0], f_sem.at[0]))
    pl.when(jnp.logical_not(at_end))(lambda: await_all(zrec, f_sem.at[0]))
    await_all(pbuf, p_sem.at[0])
    await_all(qbuf, q_sem.at[0])
    await_all(brec, b_sem.at[0])
    await_all(own_back, o_sem.at[0])
    await_all(bpar, c_sem.at[0])
    await_all(zbuf, z_sem.at[0])
    await_all(wrec, w_sem.at[0])
    await_all(wrow.at[pl.ds(0, last)], s_sem.at[0])
    await_all(wall.at[pl.ds(0, group - 1)], g_sem.at[0])
    for copy in results:
        copy.wait()


def keep_kernel(a_in, b_in, c_in, a_out, b_out, c_out, sem):
    copies = [
        pltpu.make_async_copy(src, dst, sem.at[n])
        for n, (src, dst) in enumerate([(c_in, c_out), (a_in, a_out), (b_in, b_out)])
    ]
    for copy in copies:
        copy.start()
    for copy in copies:
        copy.wait()


def local_kernel(sizes, features, weight, cotangent, block_values, block_coords, block_counts):
    nrow, ncol, nrep = sizes
    group = ncol * nrep
    every = nrow * group
    chips = group // 2
    blocks = block_values[0, 0]
    slots = blocks.shape[0]
    nodes, width = cotangent.shape
    col_nodes, fw = features.shape
    row_blocks = nodes * group // 128
    places = row_blocks * (col_nodes // 128)
    chunks = math.gcd(slots, 4)
    pieces = math.gcd(col_nodes // 128, 4)
    vmem = functools.partial(pl.BlockSpec, memory_space=pltpu.VMEM)
    hbm = functools.partial(pl.BlockSpec, memory_space=pl.ANY)
    dma = pltpu.SemaphoreType.DMA
    block = (fw, nodes)
    tile = (width * width // every // 128, 128)
    outs = pl.pallas_call(
        functools.partial(layer_kernel, sizes),
        out_shape=(
            pltpu.VMEM((nodes, width), BF16),
            pltpu.VMEM((fw, col_nodes), BF16),
            pltpu.VMEM((width, width), F32),
        ),
        in_specs=[pl.BlockSpec(memory_space=pltpu.HBM)] + [hbm()] * 5,
        out_specs=(hbm(), hbm(), hbm()),
        scratch_shapes=[
            pltpu.VMEM((nodes, width), BF16),
            pltpu.VMEM((fw, col_nodes), BF16),
            pltpu.VMEM((width, width), F32),
            pltpu.SMEM((1, 1), jnp.int32),
            pltpu.VMEM((2, slots), jnp.int32),
            pltpu.VMEM((width, width), BF16),
            pltpu.VMEM((nodes, width), BF16),
            pltpu.VMEM((nrow, pieces, fw, col_nodes // pieces), BF16),
            pltpu.VMEM((slots, 128, 128), BF16),
            pltpu.VMEM((slots + 1, 128, 128), F32),
            pltpu.VMEM((row_blocks * 128, col_nodes), BF16),
            pltpu.VMEM((nrow, chips) + block, BF16),
            pltpu.VMEM((nrow, chips) + block, BF16),
            pltpu.VMEM((nrow, chips) + block, F32),
            pltpu.VMEM((chips,) + block, F32),
            pltpu.VMEM((chips,) + block, F32),
            pltpu.VMEM((nrow, chips - 1) + block, BF16),
            pltpu.VMEM((nrow, chips - 1) + block, BF16),
            pltpu.VMEM((nrow,) + block, F32),
            pltpu.VMEM((nrow,) + block, BF16),
            pltpu.VMEM((nrow,) + block, BF16),
            pltpu.VMEM((nrow,) + block, BF16),
            pltpu.VMEM((nrow, chips - 1) + block, BF16),
            pltpu.VMEM((nrow, chips - 1) + block, BF16),
            pltpu.VMEM((nrow, fw, col_nodes), F32),
            pltpu.VMEM((nrow - 1, 4, fw // 4, col_nodes), BF16),
            pltpu.VMEM((nrow + 1, 4, fw // 4, col_nodes), BF16),
            pltpu.VMEM((every,) + tile, BF16),
            pltpu.VMEM((every - 1,) + tile, BF16),
            pltpu.VMEM((nrow,) + tile, BF16),
            pltpu.VMEM((group, nrow) + tile, BF16),
            pltpu.VMEM((1, slots + places), jnp.int32),
            pltpu.SMEM((1, slots + places), jnp.int32),
            dma((chunks,)),
            dma((8,)),
            dma,
            dma((1 + nrow * pieces,)),
            dma((1 + nrow,)),
            dma((1 + nrow,)),
            dma((1 + (nrow + 1) * (chips - 1),)),
            dma((2,)),
            dma((2 + nrow,)),
            dma((5 + nrow,)),
            dma((2,)),
            dma((2,)),
            dma((2,)),
        ],
        compiler_params=pltpu.CompilerParams(
            collective_id=0, has_side_effects=True, vmem_limit_bytes=VMEM_BUDGET
        ),
    )(block_counts, block_coords[0, 0].T, features.T, weight, cotangent, blocks)
    activations, input_grad_t, weight_grad = pl.pallas_call(
        keep_kernel,
        out_shape=tuple(jax.ShapeDtypeStruct(x.shape, x.dtype) for x in outs),
        in_specs=[hbm()] * 3,
        out_specs=(hbm(),) * 3,
        scratch_shapes=[dma((3,))],
    )(*[pltpu.with_memory_space_constraint(x, pltpu.VMEM) for x in outs])
    return activations, input_grad_t.T, weight_grad


def fits(mesh, features, weight, cotangent, block_values):
    nrow, ncol, nrep = (mesh.shape[name] for name in ("row", "col", "rep"))
    group = ncol * nrep
    width = features.shape[1]
    fw = width // nrow
    rows, cols = cotangent.shape[0] // nrow, features.shape[0] // group
    tile = rows * cols * 2 + block_values.shape[2] * 128 * 128 * 6
    moved = 8 * rows * width + 12 * cols * width
    whole = nrep % 2 == 0 and block_values.shape[2] == 128 and rows * cols % 128**3 == 0
    whole = whole and fw % 64 == 0 and width % 128 == 0 and width**2 % (2048 * nrow * group) == 0
    return whole and nrow > 3 and group > 2 and tile + moved < VMEM_BUDGET * 3 // 4


def solution(mesh):
    in_specs = (
        P(("col", "rep"), "row"),
        P(),
        P(("row", "col", "rep"), None),
        P("row", ("col", "rep"), None, None, None),
        P("row", ("col", "rep"), None, None),
        P("row", ("col", "rep")),
    )
    out_specs = (P(("row", "col", "rep"), None), P(("col", "rep"), "row"), P())
    sizes = tuple(mesh.shape[name] for name in ("row", "col", "rep"))

    def run(features, weight, cotangent, block_values, block_coords, block_counts):
        if fits(mesh, features, weight, cotangent, block_values):
            body = functools.partial(local_kernel, sizes)
        else:
            body = local_xla
        return jax.shard_map(
            body, mesh=mesh, in_specs=in_specs, out_specs=out_specs, check_vma=False
        )(features, weight, cotangent, block_values, block_coords, block_counts)

    return run
```

```python
import functools
import math

import jax
import jax.numpy as jnp
from jax import lax
from jax.experimental import pallas as pl
from jax.experimental.pallas import tpu as pltpu
from jax.sharding import PartitionSpec as P


def local_xla(features, weight, cotangent, block_values, block_coords, block_counts):
    blocks = block_values[0, 0]
    coords = block_coords[0, 0]
    live_count = block_counts[0, 0]
    slots = blocks.shape[0]
    gathered = lax.all_gather(features, "row", axis=1, tiled=True)
    feat_width = gathered.shape[1]
    col_blocks = gathered.shape[0] // 128
    row_blocks = cotangent.shape[0] * lax.axis_size(("col", "rep")) // 128
    feat_blocks = gathered.reshape(col_blocks, 128, feat_width)
    is_live = (jnp.arange(slots, dtype=jnp.int32) < live_count).astype(jnp.float32)
    per_turn = math.gcd(slots, 64)
    rounds = slots // per_turn
    pieces = (
        blocks.reshape(rounds, per_turn, 128, 128),
        coords[:, 0].reshape(rounds, per_turn),
        coords[:, 1].reshape(rounds, per_turn),
        is_live.reshape(rounds, per_turn),
    )

    def forward_step(total, piece):
        blocks_g, rows_g, cols_g, live_g = piece
        chosen = feat_blocks[cols_g]
        product = jnp.einsum("bij,bjf->bif", blocks_g, chosen, preferred_element_type=jnp.float32)
        return (total.at[rows_g].add(product * live_g[:, None, None]), None)

    partial_value, _ = lax.scan(
        forward_step, jnp.zeros((row_blocks, 128, feat_width), jnp.float32), pieces
    )
    partial_value = partial_value.reshape(row_blocks * 128, feat_width)
    summed = lax.psum_scatter(partial_value, ("col", "rep"), scatter_dimension=0, tiled=True)
    aggregate = summed.astype(jnp.bfloat16)
    pre_act = jnp.dot(aggregate, weight, preferred_element_type=jnp.float32)
    sigma = jax.nn.sigmoid(pre_act)
    activations = (pre_act * sigma).astype(jnp.bfloat16)
    grad_pre = (cotangent.astype(jnp.float32) * sigma * (1.0 + pre_act * (1.0 - sigma))).astype(
        jnp.bfloat16
    )
    weight_terms = jnp.dot(aggregate.T, grad_pre, preferred_element_type=jnp.float32)
    share = lax.psum_scatter(
        weight_terms.astype(jnp.bfloat16), ("col", "rep"), scatter_dimension=0, tiled=True
    ).astype(jnp.float32)
    share = lax.psum(share, "row")
    weight_grad = lax.all_gather(share, ("col", "rep"), axis=0, tiled=True)
    back_rows = jnp.dot(grad_pre, weight.T, preferred_element_type=jnp.float32).astype(jnp.bfloat16)
    back_all = lax.all_gather(back_rows, ("col", "rep"), axis=0, tiled=True)
    back_blocks = back_all.reshape(row_blocks, 128, back_all.shape[1])

    def backward_step(total, piece):
        blocks_g, rows_g, cols_g, live_g = piece
        chosen = back_blocks[rows_g]
        product = jnp.einsum("bji,bjf->bif", blocks_g, chosen, preferred_element_type=jnp.float32)
        return (total.at[cols_g].add(product * live_g[:, None, None]), None)

    grad_terms, _ = lax.scan(
        backward_step, jnp.zeros((col_blocks, 128, back_all.shape[1]), jnp.float32), pieces
    )
    grad_terms = grad_terms.reshape(col_blocks * 128, back_all.shape[1])
    input_grad = lax.psum_scatter(
        grad_terms.astype(jnp.bfloat16), "row", scatter_dimension=1, tiled=True
    )
    return (activations, input_grad, weight_grad)


BF16 = jnp.bfloat16
F32 = jnp.float32
VMEM_BUDGET = 60 * 2**20
MESH = pl.DeviceIdType.MESH


def dot(a, b, ca=1, cb=0):
    return lax.dot_general(a, b, (((ca,), (cb,)), ((), ())), preferred_element_type=F32)


def layer_kernel(
    sizes,
    count_hbm,
    coords_hbm,
    feat_hbm,
    weight_hbm,
    cot_hbm,
    blocks_hbm,
    act_hbm,
    igrad_hbm,
    wgrad_hbm,
    act_out,
    igrad_out,
    wgrad_out,
    count_in,
    coords_in,
    weight_in,
    cot_in,
    fbuf,
    bbuf,
    sums,
    dense,
    pbuf,
    prec,
    ownp,
    accp,
    acco,
    qbuf,
    qrec,
    held,
    agg,
    own_back,
    bown,
    brec,
    bpar,
    total,
    zbuf,
    zrec,
    wbuf,
    wrec,
    wrow,
    wall,
    tvec,
    table,
    load_sem,
    in_sem,
    t_sem,
    f_sem,
    p_sem,
    q_sem,
    o_sem,
    c_sem,
    z_sem,
    w_sem,
    s_sem,
    g_sem,
):
    nrow, ncol, nrep = sizes
    nh = nrep // 2
    group = ncol * nrep
    every = nrow * group
    slots = bbuf.shape[0]
    nodes, width = act_out.shape
    fw, col_nodes = igrad_out.shape
    pieces, cw = fbuf.shape[1], fbuf.shape[3]
    row_blocks, col_blocks = dense.shape[0] // 128, dense.shape[1] // 128
    r, c, p = lax.axis_index("row"), lax.axis_index("col"), lax.axis_index("rep")
    h, k = p // 2, p % 2
    g = c * nrep + p
    me = r * group + g
    partner = h * 2 + (1 - k)
    offsets = [(dc, dh) for dc in reversed(range(ncol)) for dh in reversed(range(nh))]
    chips = len(offsets)
    far = chips - 1
    last = nrow - 1
    at_end = (r == 0) | (r == last)
    joints = [(1, last, last - 1), (last - 1, 0, 1)]

    def to_row(j):
        return {"row": (r + j) % nrow}

    def to_group(j):
        q = (g + j) % group
        return {"col": q // nrep, "rep": q % nrep}

    def to_any(j):
        q = (me + j) % every
        return {"row": q // group, "col": q % group // nrep, "rep": q % nrep}

    def to_chip(i):
        dc, dh = offsets[i]
        return {"col": (c + dc) % ncol, "rep": ((h + dh) % nh) * 2 + k}

    def part_to(i, core):
        dc, dh = offsets[i]
        return ((c + dc) % ncol) * nrep + ((h + dh) % nh) * 2 + core

    def part_from(i, core):
        dc, dh = offsets[i]
        return ((c + ncol - dc) % ncol) * nrep + ((h + nh - dh) % nh) * 2 + core

    def by_row(choices):
        value = choices[0]
        for q in range(1, nrow):
            value = jnp.where(r == q, choices[q], value)
        return value

    def nearest(n):
        return by_row([sorted(range(nrow), key=lambda t: (abs(t - q), t))[n] for q in range(nrow)])

    def turns(q):
        rest = [t for t in range(nrow) if t != q]
        if q == 0:
            return rest[::-1] + [q]
        if q == last:
            return [0] + rest[:0:-1] + [q]
        rest.sort(key=lambda t: (abs(t - q), abs(2 * t - last)))
        for row, passed, n in joints:
            if row == q:
                rest.remove(passed)
                rest.insert(n, passed)
        return rest + [q]

    def turn(n):
        return by_row([turns(q)[n] for q in range(nrow)])

    def rcopy(src, dst, sems, n, device):
        return pltpu.make_async_remote_copy(
            src_ref=src,
            dst_ref=dst,
            send_sem=sems.at[0],
            recv_sem=sems.at[n + 1],
            device_id=device,
            device_id_type=MESH,
        )

    def await_all(ref, sem):
        pltpu.make_async_copy(ref, ref, sem).wait()

    def span(j):
        return slice(j * cw, (j + 1) * cw)

    feats = [
        pltpu.make_async_copy(feat_hbm.at[:, span(j)], fbuf.at[r, j], in_sem.at[0]) for j in range(pieces)
    ]
    others = [
        pltpu.make_async_copy(src, dst, in_sem.at[n + 1])
        for n, (src, dst) in enumerate(
            [
                (coords_hbm, coords_in),
                (count_hbm, count_in),
                (weight_hbm, weight_in),
                (cot_hbm, cot_in),
            ]
        )
    ]
    for copy in feats:
        copy.start()

    barrier = pltpu.get_barrier_semaphore()
    for j in range(1, nrow):
        pl.semaphore_signal(barrier, inc=1, device_id=to_row(j), device_id_type=MESH)
    for j in range(1, group):
        pl.semaphore_signal(barrier, inc=1, device_id=to_group(j), device_id_type=MESH)
    for copy in others[:2]:
        copy.start()
    chunks = load_sem.shape[0]
    per = slots // chunks
    loads = []
    for i in range(chunks):
        there = pl.ds(i * per, per)
        loads.append(pltpu.make_async_copy(blocks_hbm.at[there], bbuf.at[there], load_sem.at[i]))
        loads[-1].start()
    for copy in others[2:]:
        copy.start()
    await_all(fbuf.at[r], in_sem.at[0])
    pl.semaphore_wait(barrier, nrow - 1 + group - 1)

    def feat_copy(src, slot, j, step):
        target = {"row": (r + nrow + step) % nrow}
        return rcopy(src, fbuf.at[slot, j], f_sem, slot * pieces + j, target)

    for j in range(pieces):
        for step, there in ((1, r < last), (-1, r > 0)):
            pl.when(there)(feat_copy(fbuf.at[r, j], r, j, step).start)

    def relay(d, j):
        for slot, step, there in (
            (jnp.maximum(r - d, 0), 1, (r >= d) & (r < last)),
            (jnp.minimum(r + d, last), -1, (r + d <= last) & (r > 0)),
        ):

            @pl.when(there)
            def _(slot=slot, step=step):
                copy = feat_copy(fbuf.at[slot, j], slot, j, step)
                copy.wait_recv()
                copy.start()

    for copy in others[:2]:
        copy.wait()
    places = row_blocks * col_blocks
    live = count_in[0, 0]
    row_form = coords_in[0:1, :] * col_blocks + coords_in[1:2, :]
    column_form = jnp.broadcast_to(row_form, (slots, slots)).T
    mine_at = lax.broadcasted_iota(jnp.int32, (slots, slots), 0)
    other_at = lax.broadcasted_iota(jnp.int32, (slots, slots), 1)
    hit = (column_form == row_form) & (mine_at < jnp.minimum(other_at, live))
    tvec[0:1, 0:slots] = jnp.max(jnp.where(hit, mine_at + 1, 0), axis=0, keepdims=True)
    for start in range(0, places, slots):
        hit = (column_form == other_at + start) & (mine_at < live)
        tvec[0:1, slots + start : 2 * slots + start] = jnp.max(
            jnp.where(hit, mine_at + 1, 0), axis=0, keepdims=True
        )
    tcopy = pltpu.make_async_copy(tvec, table, t_sem)
    tcopy.start()
    tcopy.wait()

    sums[0] = jnp.zeros((128, 128), F32)
    for i in range(chunks):
        loads[i].wait()

        def add_slot(s, carry):
            sums[s + 1] = sums[table[0, s]] + bbuf[s].astype(F32)
            return carry

        lax.fori_loop(i * per, (i + 1) * per, add_slot, 0)

    def fill(rb, carry):
        for cb in range(col_blocks):
            block = sums[table[0, slots + rb * col_blocks + cb]]
            dense[pl.ds(rb * 128, 128), cb * 128 : (cb + 1) * 128] = block.astype(BF16)
        return carry

    lax.fori_loop(0, row_blocks, fill, 0)

    def partials(n, core, reach):
        slot, (low, high) = nearest(n), reach
        rows = jnp.concatenate([fbuf[slot, j] for j in range(low, high)], axis=1)
        parts = [part_to(i, core) for i in range(chips)]
        cols = slice(low * cw, high * cw)
        return [dot(rows, dense[pl.ds(part * nodes, nodes), cols], 1, 1) for part in parts]

    def tail(n):
        return (0 if n < last else pieces - 1, pieces)

    def merge(n):
        pcopies[n].wait_recv()
        for i in range(chips):
            both = ownp[n, i] + prec[n, i].astype(F32)
            if i == far:
                held[n] = both
            else:
                qbuf[n, i] = both.astype(BF16)
                rcopy(qbuf.at[n, i], qrec.at[n, i], q_sem, n, to_chip(i)).start()

    def collect(n):
        await_all(qrec.at[n], q_sem.at[n + 1])
        got = held[n]
        for i in range(far):
            got = got + qrec[n, i].astype(F32)
        agg[nearest(n)] = got.astype(BF16)

    relays = [(d, j) for d in range(1, nrow - 1) for j in range(pieces)]
    when = [min((0, 1, 2, 2, 3, 4, 4, 5)[n % 8] + n // 8 * 4, 2 * nrow - 2) for n in range(len(relays))]
    pcopies = []
    for n in range(nrow):
        for half in range(2):
            for at, (d, j) in zip(when, relays):
                if at == 2 * n + half:
                    relay(d, j)
            if half == 0:
                if n > 0:
                    slot = nearest(n)
                    for j in range(pieces):
                        copy = feat_copy(fbuf.at[slot, j], slot, j, 0)
                        pl.when(at_end)(copy.wait_recv)
                        if n == last and 0 < j < pieces - 1:
                            for core, sofar in ((1 - k, accp), (k, acco)):
                                for i, part in enumerate(partials(n, core, (0 if j == 1 else j, j + 1))):
                                    sofar[i] = part if j == 1 else sofar[i] + part
                for i, part in enumerate(partials(n, 1 - k, tail(n))):
                    pbuf[n, i] = (part if n < last else accp[i] + part).astype(BF16)
                pcopies.append(rcopy(pbuf.at[n], prec.at[n], p_sem, n, {"rep": partner}))
                pcopies[n].start()
            else:
                for i, part in enumerate(partials(n, k, tail(n))):
                    ownp[n, i] = part if n < last else acco[i] + part
                merge(n)
                if n > 1:
                    collect(n - 2)

    for copy in others[2:]:
        copy.wait()
    pl.when(at_end)(lambda: await_all(fbuf.at[0], f_sem.at[0]))
    pl.when(jnp.logical_not(at_end))(lambda: await_all(zrec, f_sem.at[0]))
    collect(last - 1)
    collect(last)

    aggregate = agg[...].reshape(width, nodes)
    pre_act = dot(aggregate, weight_in[...], 0, 0)
    sigma = jax.nn.sigmoid(pre_act)
    grad_pre = (cot_in[...].astype(F32) * sigma * (1.0 + pre_act * (1.0 - sigma))).astype(BF16)
    own_back[...] = dot(weight_in[...], grad_pre, 1, 1).astype(BF16).reshape(nrow, fw, nodes)

    units = [(0, m, fw // 2) for m in (0, fw // 2)] + [(n, 0, fw) for n in range(1, nrow)]

    def spread(u):
        n, at, size = units[u]
        rows = pl.ds(at, size)
        for i in range(far):
            src, dst = own_back.at[turn(n), rows], brec.at[n, i, rows]
            rcopy(src, dst, f_sem, u * far + i, to_chip(i)).start()

    ocopy = rcopy(own_back, bown, o_sem, 0, {"rep": partner})
    spread(0)
    ocopy.start()
    spread(1)
    spread(2)
    terms = dot(aggregate, grad_pre).astype(BF16)
    tr, tl = wbuf.shape[1:]
    wbuf[...] = jnp.concatenate(
        [terms[:, n * tl : (n + 1) * tl].reshape(width // tr, tr, tl) for n in range(width // tl)], axis=0
    )
    for j in range(1, every):
        rcopy(wbuf.at[(me + j) % every], wrec.at[j - 1], w_sem, 0, to_any(j)).start()
    for u in range(3, len(units)):
        spread(u)
    act_out[...] = (pre_act * sigma).astype(BF16)
    results = [
        pltpu.make_async_copy(src, dst, load_sem.at[n])
        for n, (src, dst) in enumerate(
            [(act_out, act_hbm), (igrad_out, igrad_hbm), (wgrad_out, wgrad_hbm)]
        )
    ]
    results[0].start()

    def back_term(piece_t, part):
        return dot(piece_t, dense[pl.ds(part * nodes, nodes), :])

    def begin(n):
        total[n] = back_term(own_back[turn(n)], g) + back_term(bown[turn(n)], c * nrep + partner)

    def middle(u):
        n, at, size = units[u]
        rows = pl.ds(at, size)
        for i in reversed(range(far)):
            copy = rcopy(brec.at[n, i, rows], bpar.at[n, i, rows], c_sem, u, {"rep": partner})
            await_all(brec.at[n, i, rows], f_sem.at[u * far + i + 1])
            copy.start()
            total[n, rows] += back_term(brec[n, i, rows], part_from(i, k))

    def finish(u):
        n, at, size = units[u]
        rows = pl.ds(at, size)
        await_all(bpar.at[n, :, rows], c_sem.at[u + 1])
        for i in reversed(range(far)):
            total[n, rows] += back_term(bpar[n, i, rows], part_from(i, 1 - k))

    steps = zbuf.shape[1]
    fh = fw // steps

    def zpart(n, m):
        return total[n, m * fh : (m + 1) * fh]

    def zcopy(n, m):
        q = turn(n)
        far_off = jnp.abs(q - r) == last
        inner = jnp.where(r == 0, 1, last - 1)
        lane = jnp.where(far_off, nrow, r)
        target = {"row": jnp.where(far_off, inner, q)}
        return rcopy(zbuf.at[n, m], zrec.at[lane, m], z_sem, lane + jnp.where(far_off, m, 0), target)

    ocopy.wait_recv()
    begin(0)

    def join(n, span):
        for row, _, at in joints:
            if at == n:

                @pl.when(r == row)
                def _():
                    for m in span:
                        await_all(zrec.at[nrow, m], z_sem.at[nrow + m + 1])
                        zbuf[n, m] = (zpart(n, m) + zrec[nrow, m].astype(F32)).astype(BF16)
                        zcopy(n, m).start()

    def advance(u):
        if u < len(units):
            if units[u][1] == 0 and u > 0:
                begin(units[u][0])
            middle(u)

    middle(0)
    for u, (n, at, size) in enumerate(units):
        pl.when(k == 1)(lambda: advance(u + 1))
        if u > 0 and n > 0:
            join(n - 1, range(steps // 2))
        finish(u)
        if n == 1:
            await_all(wrec, w_sem.at[1])
            share = wbuf[me].astype(F32)
            for j in range(every - 1):
                share = share + wrec[j].astype(F32)
            wrow[r] = share.astype(BF16)
            for j in range(1, nrow):
                rcopy(wrow.at[r], wrow.at[r], s_sem, 0, to_row(j)).start()
        if n < last:

            def put(n=n, at=at, size=size):
                for m in range(at // fh, (at + size) // fh):
                    zbuf[n, m] = zpart(n, m).astype(BF16)
                    zcopy(n, m).start()

            keep = functools.reduce(jnp.logical_and, [r != row for row, _, at in joints if at == n], r >= 0)
            pl.when(keep)(put)
        pl.when(k == 0)(lambda: advance(u + 1))
        if n > 0:
            join(n - 1, range(steps // 2, steps))

    await_all(wrow.at[pl.ds(0, last)], s_sem.at[1])
    wall[g] = wrow[...]
    for j in range(1, group):
        rcopy(wrow, wall.at[g], g_sem, 0, to_group(j)).start()

    for j in range(1, nrow):
        q = (r + j) % nrow

        @pl.when(jnp.abs(q - r) < last)
        def _(q=q):
            await_all(zrec.at[q], z_sem.at[q + 1])
            for m in range(steps):
                total[last, m * fh : (m + 1) * fh] += zrec[q, m].astype(F32)

    igrad_out[...] = total[last].astype(BF16)
    results[1].start()
    await_all(wall.at[pl.ds(0, group - 1)], g_sem.at[1])
    per_lane = width // tr
    for row in range(nrow):
        for q in range(group):
            n = row * group + q
            at, lane = n % per_lane * tr, n // per_lane * tl
            wgrad_out[at : at + tr, lane : lane + tl] = wall[q, row].astype(F32)
    results[2].start()
    await_all(pbuf, p_sem.at[0])
    await_all(qbuf, q_sem.at[0])
    await_all(brec, f_sem.at[0])
    await_all(own_back, o_sem.at[0])
    await_all(bpar, c_sem.at[0])
    await_all(zbuf, z_sem.at[0])
    await_all(wrec, w_sem.at[0])
    await_all(wrow.at[pl.ds(0, last)], s_sem.at[0])
    await_all(wall.at[pl.ds(0, group - 1)], g_sem.at[0])
    for copy in results:
        copy.wait()


def keep_kernel(a_in, b_in, c_in, a_out, b_out, c_out, sem):
    copies = [
        pltpu.make_async_copy(src, dst, sem.at[n])
        for n, (src, dst) in enumerate([(c_in, c_out), (a_in, a_out), (b_in, b_out)])
    ]
    for copy in copies:
        copy.start()
    for copy in copies:
        copy.wait()


def local_kernel(sizes, features, weight, cotangent, block_values, block_coords, block_counts):
    nrow, ncol, nrep = sizes
    group = ncol * nrep
    every = nrow * group
    chips = group // 2
    blocks = block_values[0, 0]
    slots = blocks.shape[0]
    nodes, width = cotangent.shape
    col_nodes, fw = features.shape
    row_blocks = nodes * group // 128
    places = row_blocks * (col_nodes // 128)
    chunks = math.gcd(slots, 4)
    pieces = math.gcd(col_nodes // 128, 4)
    vmem = functools.partial(pl.BlockSpec, memory_space=pltpu.VMEM)
    hbm = functools.partial(pl.BlockSpec, memory_space=pl.ANY)
    dma = pltpu.SemaphoreType.DMA
    block = (fw, nodes)
    tile = (width * width // every // 128, 128)
    outs = pl.pallas_call(
        functools.partial(layer_kernel, sizes),
        out_shape=(
            pltpu.VMEM((nodes, width), BF16),
            pltpu.VMEM((fw, col_nodes), BF16),
            pltpu.VMEM((width, width), F32),
        ),
        in_specs=[pl.BlockSpec(memory_space=pltpu.HBM)] + [hbm()] * 5,
        out_specs=(hbm(), hbm(), hbm()),
        scratch_shapes=[
            pltpu.VMEM((nodes, width), BF16),
            pltpu.VMEM((fw, col_nodes), BF16),
            pltpu.VMEM((width, width), F32),
            pltpu.SMEM((1, 1), jnp.int32),
            pltpu.VMEM((2, slots), jnp.int32),
            pltpu.VMEM((width, width), BF16),
            pltpu.VMEM((nodes, width), BF16),
            pltpu.VMEM((nrow, pieces, fw, col_nodes // pieces), BF16),
            pltpu.VMEM((slots, 128, 128), BF16),
            pltpu.VMEM((slots + 1, 128, 128), F32),
            pltpu.VMEM((row_blocks * 128, col_nodes), BF16),
            pltpu.VMEM((nrow, chips) + block, BF16),
            pltpu.VMEM((nrow, chips) + block, BF16),
            pltpu.VMEM((nrow, chips) + block, F32),
            pltpu.VMEM((chips,) + block, F32),
            pltpu.VMEM((chips,) + block, F32),
            pltpu.VMEM((nrow, chips - 1) + block, BF16),
            pltpu.VMEM((nrow, chips - 1) + block, BF16),
            pltpu.VMEM((nrow,) + block, F32),
            pltpu.VMEM((nrow,) + block, BF16),
            pltpu.VMEM((nrow,) + block, BF16),
            pltpu.VMEM((nrow,) + block, BF16),
            pltpu.VMEM((nrow, chips - 1) + block, BF16),
            pltpu.VMEM((nrow, chips - 1) + block, BF16),
            pltpu.VMEM((nrow, fw, col_nodes), F32),
            pltpu.VMEM((nrow - 1, 4, fw // 4, col_nodes), BF16),
            pltpu.VMEM((nrow + 1, 4, fw // 4, col_nodes), BF16),
            pltpu.VMEM((every,) + tile, BF16),
            pltpu.VMEM((every - 1,) + tile, BF16),
            pltpu.VMEM((nrow,) + tile, BF16),
            pltpu.VMEM((group, nrow) + tile, BF16),
            pltpu.VMEM((1, slots + places), jnp.int32),
            pltpu.SMEM((1, slots + places), jnp.int32),
            dma((chunks,)),
            dma((5,)),
            dma,
            dma((1 + max(nrow * pieces, (nrow + 1) * (chips - 1)),)),
            dma((1 + nrow,)),
            dma((1 + nrow,)),
            dma((2,)),
            dma((2 + nrow,)),
            dma((5 + nrow,)),
            dma((2,)),
            dma((2,)),
            dma((2,)),
        ],
        compiler_params=pltpu.CompilerParams(
            collective_id=0, has_side_effects=True, vmem_limit_bytes=VMEM_BUDGET
        ),
    )(block_counts, block_coords[0, 0].T, features.T, weight, cotangent, blocks)
    activations, input_grad_t, weight_grad = pl.pallas_call(
        keep_kernel,
        out_shape=tuple(jax.ShapeDtypeStruct(x.shape, x.dtype) for x in outs),
        in_specs=[hbm()] * 3,
        out_specs=(hbm(),) * 3,
        scratch_shapes=[dma((3,))],
    )(*[pltpu.with_memory_space_constraint(x, pltpu.VMEM) for x in outs])
    return activations, input_grad_t.T, weight_grad


def fits(mesh, features, weight, cotangent, block_values):
    nrow, ncol, nrep = (mesh.shape[name] for name in ("row", "col", "rep"))
    group = ncol * nrep
    width = features.shape[1]
    fw = width // nrow
    rows, cols = cotangent.shape[0] // nrow, features.shape[0] // group
    tile = rows * cols * 2 + block_values.shape[2] * 128 * 128 * 6
    moved = 8 * rows * width + 12 * cols * width
    whole = nrep % 2 == 0 and block_values.shape[2] == 128 and rows * cols % 128**3 == 0
    whole = whole and fw % 64 == 0 and width % 128 == 0 and width**2 % (2048 * nrow * group) == 0
    return whole and nrow > 3 and group > 2 and tile + moved < VMEM_BUDGET * 3 // 4


def solution(mesh):
    in_specs = (
        P(("col", "rep"), "row"),
        P(),
        P(("row", "col", "rep"), None),
        P("row", ("col", "rep"), None, None, None),
        P("row", ("col", "rep"), None, None),
        P("row", ("col", "rep")),
    )
    out_specs = (P(("row", "col", "rep"), None), P(("col", "rep"), "row"), P())
    sizes = tuple(mesh.shape[name] for name in ("row", "col", "rep"))

    def run(features, weight, cotangent, block_values, block_coords, block_counts):
        if fits(mesh, features, weight, cotangent, block_values):
            body = functools.partial(local_kernel, sizes)
        else:
            body = local_xla
        return jax.shard_map(
            body, mesh=mesh, in_specs=in_specs, out_specs=out_specs, check_vma=False
        )(features, weight, cotangent, block_values, block_coords, block_counts)

    return run
```
